256 devices in a mesh: row: 4 (over y_lo, core), col: 64 (over z, y_hi, x).
Axes of the slice: x: 4, y: 4 (y_hi: 2, y_lo: 2; y = y_hi * 2 + y_lo), z: 8, core: 2. Of those that a mesh axis runs over, the one named last changes fastest.
Arguments:
- state: bfloat16 [65536, 144], P('col', 'row'), may hold values from -6 to 6
- adjoint: bfloat16 [65536, 144], P('col', 'row'), may hold values from -6 to 6
- area: float32 [65536], P('col'), may hold values from 0.5 to 4
- node_coords: bfloat16 [3, 32768], P(None, 'col'), may hold values from 0 to 4
- connect: int32 [3, 65536], P(None, 'col'), may hold values from 0 to 32767, as said below
- front_list: int32 [4096], P('row'), may hold values from 0 to 65535, as said below
- tile_class: int32 [16, 256], P('row', 'col'), may hold values from 0 to 1, as said below
Outputs:
- front_grad: float32 [4096, 48], P(('row', 'col'))
- node_grad: float32 [32768, 48], P('col')
The draws below stay inside these ranges and needn't reach their ends.
Inputs may be any that keep to these rules, and one draw needn't show every extreme that they name: `connect`: the three numbers of element j are distinct nodes of block j // 1024, that is within [(j // 1024) * 512, (j // 1024 + 1) * 512). `front_list`: distinct element numbers; the last element is among them. `tile_class`: 0 selects the one-point (centroid) rule, 1 the three-point (vertex) rule; every tile within the 1024 surface elements of some index of col has class 1.
All inputs are finite; a program needn't handle non-finite values.
Results may differ from the reference program's by a relative error of at most 0.009.
Values may be sent and summed in bfloat16 or wider, within the bound.
No kernel may reach another device: no remote copies, remote signals or barrier semaphores. Data moves between devices by JAX's collectives and lax.ppermute only.
A program may use at most 64 MiB of HBM per device.

```python
import math
import jax
import jax.numpy as jnp
from jax import lax

CH = 144
E_DEV = 1024
TR = 256
TC = 256
NODE_DEV = 512
FRONT = 4096
ELEMS = 65536
NODES = 32768


def draw_connect(key, part):
    first_key, second_key, third_key = jax.random.split(jax.random.fold_in(key, 11), 3)
    half = NODE_DEV // 2
    base = jax.random.randint(first_key, (ELEMS,), 0, NODE_DEV)
    near = jax.random.randint(second_key, (ELEMS,), 0, half)
    far = jax.random.randint(third_key, (ELEMS,), 0, NODE_DEV - half - 1)
    second = (base + 1 + near) % NODE_DEV
    third = (base + half + 1 + far) % NODE_DEV
    shard = jnp.arange(ELEMS, dtype=jnp.int32) // E_DEV
    local = jnp.stack([base, second, third])
    return (local + shard[None, :] * NODE_DEV).astype(jnp.int32)


def draw_front_list(key, part):
    shuffled = jax.random.permutation(jax.random.fold_in(key, 23), ELEMS).astype(jnp.int32)
    where_last = jnp.argmax(shuffled == ELEMS - 1).astype(jnp.int32)
    return jnp.roll(shuffled, -where_last)[:FRONT].astype(jnp.int32)


def draw_tile_class(key, part):
    rate_key, pick_key, roll_key = jax.random.split(jax.random.fold_in(key, 37), 3)
    groups = ELEMS // E_DEV
    per_group = E_DEV // TC
    rates = jax.random.randint(rate_key, (groups,), 0, 9)
    busiest = jax.random.randint(pick_key, (), 0, groups)
    rates = jnp.where(jnp.arange(groups) == busiest, 8, rates)
    rolls = jax.random.randint(roll_key, (FRONT // TR, ELEMS // TC), 0, 8)
    owner = jnp.arange(ELEMS // TC) // per_group
    return (rolls < rates[owner][None, :]).astype(jnp.int32)


def shard_levels(stream_key, extent, cuts, least, top_value):
    level, own = 1.0, jax.random.fold_in(stream_key, 6)
    for position, shards_of in cuts:
        steps = jnp.exp(jax.random.uniform(jax.random.fold_in(own, position), (shards_of,), jnp.float32, least / len(cuts), top_value / len(cuts)))
        level = level * jnp.repeat(steps, extent[position] // shards_of).reshape([-1 if axis == position else 1 for axis in range(len(extent))])
    return level


def normal_values(key, dims, deviation, limit, cuts=(), kind=jnp.bfloat16):
    array = jax.random.normal(key, dims, jnp.float32) * deviation
    if len(cuts) > 0:
        array = shard_levels(key, dims, cuts, -0.22, 0.18) * array
    return jnp.clip(array, min=-limit, max=limit).astype(kind)


def setup_inputs(seed: int = 0) -> dict:
    keys = jax.random.split(jax.random.key(seed), 8)
    state = normal_values(keys[0], (ELEMS, CH), 1.0, 6.0, ((0, 64), (1, 4)))
    adjoint = normal_values(keys[1], (ELEMS, CH), 1.0, 6.0, ((0, 64), (1, 4)))
    area = jnp.clip(jnp.exp(math.log(4.0) - 2.0794415 * jax.random.uniform(keys[2], (ELEMS,), jnp.float32) ** shard_levels(keys[2], (ELEMS,), ((0, 64),), -0.2, 0.2)), 0.5, 4.0)
    node_coords = jnp.clip(4.0 * jax.random.uniform(keys[3], (3, NODES), jnp.float32) ** shard_levels(keys[3], (3, NODES), ((1, 64),), -0.2, 0.2), 0.0, 4.0).astype(jnp.bfloat16)
    connect = draw_connect(jax.random.fold_in(keys[7], 71), 0)
    front_list = draw_front_list(jax.random.fold_in(keys[7], 71), 0)
    tile_class = draw_tile_class(jax.random.fold_in(keys[7], 71), 0)
    return {"state": state, "adjoint": adjoint, "area": area, "node_coords": node_coords, "connect": connect, "front_list": front_list, "tile_class": tile_class}


SOFTEN = 0.05

def pair_sum(leader, product):
    count = leader.shape[0]
    joined = leader.astype(jnp.float32) * product
    return lax.optimization_barrier(jnp.sum(joined.reshape(count, 2, -1, 9), axis=(1, 3)))

def kernel_rows(front_x, positions, weight):
    offsets = [front_x[direction][:, None] - positions[direction][None, :] for direction in range(3)]
    squared = offsets[0] * offsets[0] + offsets[1] * offsets[1] + offsets[2] * offsets[2] + SOFTEN
    factor = weight[None, :] / (squared * jnp.sqrt(squared))
    return [(offsets[direction] * factor).astype(jnp.bfloat16) for direction in range(3)]

def row_terms(summed, front_pack, col_pack):
    pieces = []
    for direction in range(3):
        product = jnp.dot(summed[direction], col_pack, preferred_element_type=jnp.float32)
        pieces.append(-pair_sum(front_pack, product))
    return jnp.concatenate(pieces, 1)

def col_terms(kernels, front_pack, col_pack):
    pieces = []
    for direction in range(3):
        product = lax.dot_general(kernels[direction], front_pack, (((0,), (0,)), ((), ())), preferred_element_type=jnp.float32)
        pieces.append(pair_sum(col_pack, product))
    return jnp.concatenate(pieces, 1)

def one_point(front_x, front_pack, points, center, weight, col_pack):
    kernels = kernel_rows(front_x, center, weight)
    summed = [(kernel.astype(jnp.float32) * 3.0).astype(jnp.bfloat16) for kernel in kernels]
    row_part = row_terms(summed, front_pack, col_pack)
    node_slot = col_terms(kernels, front_pack, col_pack)
    return (row_part, jnp.concatenate([node_slot, node_slot, node_slot], 1))

def three_point(front_x, front_pack, points, center, weight, col_pack):
    per_node = [kernel_rows(front_x, points[corner], weight) for corner in range(3)]
    summed = [(per_node[0][direction].astype(jnp.float32) + per_node[1][direction].astype(jnp.float32) + per_node[2][direction].astype(jnp.float32)).astype(jnp.bfloat16) for direction in range(3)]
    row_part = row_terms(summed, front_pack, col_pack)
    slots = [col_terms(per_node[corner], front_pack, col_pack) for corner in range(3)]
    return (row_part, jnp.concatenate(slots, 1))

def tile_sweep(front_x, front_pack, points, center, weight, col_pack, tile_class):
    front_count = front_pack.shape[0]
    elem_count = col_pack.shape[0]
    row_tiles = tile_class.shape[0]
    col_tiles = tile_class.shape[1]
    tile_rows = front_count // row_tiles
    tile_cols = elem_count // col_tiles
    load_count = col_pack.shape[1] // 18
    row_zero = jnp.zeros((front_count, 3 * load_count), jnp.float32)
    col_zero = jnp.zeros((elem_count, 9 * load_count), jnp.float32)

    def visit(counter, carry):
        row_total, col_total = carry
        tile_row = counter // col_tiles
        tile_col = counter % col_tiles
        row_start = (tile_row * tile_rows).astype(jnp.int32)
        col_start = (tile_col * tile_cols).astype(jnp.int32)
        tile_front = lax.dynamic_slice_in_dim(front_x, row_start, tile_rows, 1)
        tile_pack = lax.dynamic_slice_in_dim(front_pack, row_start, tile_rows, 0)
        tile_points = lax.dynamic_slice_in_dim(points, col_start, tile_cols, 2)
        tile_center = lax.dynamic_slice_in_dim(center, col_start, tile_cols, 1)
        tile_weight = lax.dynamic_slice_in_dim(weight, col_start, tile_cols, 0)
        tile_columns = lax.dynamic_slice_in_dim(col_pack, col_start, tile_cols, 0)
        tile_kind = tile_class[tile_row, tile_col]
        row_part, col_part = lax.cond(tile_kind == 1, three_point, one_point, tile_front, tile_pack, tile_points, tile_center, tile_weight, tile_columns)
        row_total = lax.dynamic_update_slice_in_dim(row_total, lax.dynamic_slice_in_dim(row_total, row_start, tile_rows, 0) + row_part, row_start, 0)
        col_total = lax.dynamic_update_slice_in_dim(col_total, lax.dynamic_slice_in_dim(col_total, col_start, tile_cols, 0) + col_part, col_start, 0)
        return (row_total, col_total)
    return lax.fori_loop(0, row_tiles * col_tiles, visit, (row_zero, col_zero))

def reference(state, adjoint, area, node_coords, connect, front_list, tile_class):
    coords = node_coords.astype(jnp.float32)
    points = jnp.stack([coords[:, connect[corner]] for corner in range(3)])
    center = (points[0] + points[1] + points[2]) / 3.0
    weight = area * ((FRONT * ELEMS) ** (-0.25) / 3.0)
    col_pack = jnp.concatenate([state, adjoint], 1)
    front_pack = jnp.concatenate([adjoint[front_list], state[front_list]], 1)
    front_x = center[:, front_list]
    front_grad, elem_grad = tile_sweep(front_x, front_pack, points, center, weight, col_pack, tile_class)
    node_grad = jax.ops.segment_sum(elem_grad.reshape(ELEMS * 3, -1), connect.T.reshape(-1), num_segments=NODES)
    return (front_grad, node_grad)
```

```python
import jax
import jax.numpy as jnp
from jax import lax
from jax.experimental import pallas as pl
from jax.experimental.pallas import tpu as pltpu
from jax.sharding import Mesh, PartitionSpec as P

SOFTEN = 0.05
COL = ("z", "yh", "x")
ROW = ("yl", "co")
BF = jnp.bfloat16
F32 = jnp.float32

NT = (((1,), (1,)), ((), ()))


def iota(shape, dim):
    return lax.broadcasted_iota(jnp.int32, shape, dim)


def one_hot(mask):
    return jnp.where(mask, 1.0, 0.0).astype(BF)


def prep_kernel(gathered_ref, connect_ref, coords_ref, local_ref, pack_ref, points_ref, rows_ref):
    place = iota((288, 320), 0)
    source = iota((288, 320), 1)
    group = place >> 4
    load = place & 15
    half = jnp.where(group >= 9, 1, 0)
    comp = group - 9 * half
    wanted = (load >> 2) * 80 + half * 36 + (load & 3) * 9 + comp
    permute = one_hot(source == wanted)
    gathered = gathered_ref[...].reshape(320, 1024)
    pack = jnp.dot(permute, gathered, preferred_element_type=F32).astype(BF)
    pack_ref[...] = pack
    points = jnp.zeros((16, 1024), F32)
    for corner in range(3):
        chosen = one_hot(iota((512, 1024), 0) == connect_ref[corner : corner + 1, :])
        points = points + jnp.dot(coords_ref[corner], chosen, preferred_element_type=F32)
    points_ref[...] = points
    table = jnp.concatenate([pack[144:], pack[:144], points.astype(BF)], 0)
    owned = one_hot(iota((1024, 1024), 0) == local_ref[...])
    picked = jnp.dot(table, owned, preferred_element_type=F32)
    picked = jnp.concatenate([picked, jnp.zeros((80, 1024), F32)], 0)
    rows_ref[...] = jnp.transpose(picked).astype(BF)


def main_kernel(
    class_ref,
    pack_ref,
    points_ref,
    area_ref,
    connect_ref,
    rows_ref,
    front_ref,
    node_ref,
    kern_ref,
    dsum_ref,
    frontx_ref,
    fpack_ref,
    elem_ref,
):
    scale = (4096 * 65536) ** (-0.25) / 3.0
    weight = area_ref[...] * scale
    rows = rows_ref[...].astype(F32)
    fpack_ref[...] = jnp.transpose(rows)[:288].astype(BF)
    tail = rows[:, 256:384]
    for k in range(3):
        value = (tail[:, 32 + k : 33 + k] + tail[:, 35 + k : 36 + k] + tail[:, 38 + k : 39 + k]) / 3.0
        frontx_ref[k] = jnp.broadcast_to(value, (1024, 128))
    points = [[points_ref[3 * a + k : 3 * a + k + 1, :] for k in range(3)] for a in range(3)]
    center = [(points[0][k] + points[1][k] + points[2][k]) / 3.0 for k in range(3)]

    for jt in range(4):
        cols = slice(256 * jt, 256 * jt + 256)
        wide = weight[:, cols]
        for it in range(4):
            vertex = class_ref[it, jt] == 1
            place = [
                [jnp.where(vertex, points[a][k][:, cols], center[k][:, cols]) for k in range(3)]
                for a in range(3)
            ]

            def chunk(step, carry):
                start = pl.multiple_of(256 * it + 16 * step, 16)
                at = pl.ds(start, 16)
                front = []
                for k in range(3):
                    piece = frontx_ref[k, at, :]
                    front.append(jnp.concatenate([piece, piece], 1))
                total = [None] * 3
                for a in range(3):
                    offset = [front[k] - place[a][k] for k in range(3)]
                    squared = (
                        offset[0] * offset[0] + offset[1] * offset[1] + offset[2] * offset[2] + SOFTEN
                    )
                    inverse = lax.rsqrt(squared)
                    factor = (wide * inverse) * (inverse * inverse)
                    for k in range(3):
                        value = offset[k] * factor
                        kern_ref[3 * a + k, at, :] = value.astype(BF)
                        total[k] = value if a == 0 else total[k] + value
                for k in range(3):
                    dsum_ref[k, at, cols] = total[k].astype(BF)
                return carry

            lax.fori_loop(0, 16, chunk, 0)
        leader = pack_ref[:, cols].astype(F32)
        for ak in range(9):
            product = jnp.dot(fpack_ref[...], kern_ref[ak], preferred_element_type=F32)
            joined = (product * leader).reshape(18, 16, 256)
            elem_ref[16 * ak : 16 * ak + 16, cols] = jnp.sum(joined, axis=0)

    pieces = []
    for k in range(3):
        product = lax.dot_general(pack_ref[...], dsum_ref[k], NT, preferred_element_type=F32)
        joined = (product * fpack_ref[...].astype(F32)).reshape(18, 16, 1024)
        pieces.append(-jnp.sum(joined, axis=0))
    pieces.append(jnp.zeros((80, 1024), F32))
    turned = jnp.transpose(jnp.concatenate(pieces, 0)).reshape(64, 16, 128)
    packed = turned[:, :8] + pltpu.roll(turned[:, 8:].reshape(512, 128), 64, 1).reshape(64, 8, 128)
    front_ref[...] = packed.astype(BF)

    nodes = jnp.zeros((96, 512), F32)
    for a in range(3):
        value = elem_ref[48 * a : 48 * a + 48, :]
        high = value.astype(BF)
        low = (value - high.astype(F32)).astype(BF)
        chosen = one_hot(iota((512, 1024), 0) == connect_ref[a : a + 1, :])
        nodes = nodes + lax.dot_general(
            jnp.concatenate([high, low], 0), chosen, NT, preferred_element_type=F32
        )
    node_ref[...] = (nodes[:48] + nodes[48:]).astype(BF)


def last_kernel(front_ref, own_ref, core_ref, side_ref, cross_ref, out_front_ref, out_node_ref):
    total = jnp.sum(front_ref[...].astype(F32), axis=0)
    out_front_ref[0:8, :] = total[:, 0:48]
    out_front_ref[8:16, :] = pltpu.roll(total, 64, 1)[:, 0:48]
    near = own_ref[...].astype(F32) + core_ref[...].astype(F32)
    far = side_ref[...].astype(F32) + cross_ref[...].astype(F32)
    out_node_ref[...] = near + far


def shape(dims, dtype):
    return jax.ShapeDtypeStruct(dims, dtype)


VMEM = pl.BlockSpec(memory_space=pltpu.VMEM)
SMEM = pl.BlockSpec(memory_space=pltpu.SMEM)


def body(state, adjoint, area, node_coords, connect, front_list, tile_class):
    col_index = lax.axis_index(COL)
    mine = jnp.concatenate([state.T, adjoint.T, jnp.zeros((8, 1024), BF)], 0)
    gathered = lax.all_gather(mine, ROW)
    connect = connect - col_index * 512
    local = (front_list - col_index * 1024).reshape(1, 1024)
    coords = jnp.stack([jnp.pad(node_coords, ((3 * a, 13 - 3 * a), (0, 0))) for a in range(3)])
    pack, points, rows = pl.pallas_call(
        prep_kernel,
        out_shape=(shape((288, 1024), BF), shape((16, 1024), F32), shape((1024, 384), BF)),
        in_specs=[VMEM] * 4,
        out_specs=(VMEM, VMEM, VMEM),
        name="prep",
    )(gathered, connect, coords, local)
    part = lax.all_to_all(rows.reshape(64, 16, 384), COL, 0, 0)
    share = jnp.sum(part, axis=0, dtype=BF)
    spread = jnp.broadcast_to(share[None], (64, 16, 384))
    front_rows = lax.all_to_all(spread, COL, 0, 0).reshape(1024, 384)
    front_part, node_part = pl.pallas_call(
        main_kernel,
        out_shape=(shape((64, 8, 128), BF), shape((48, 512), BF)),
        in_specs=[SMEM] + [VMEM] * 5,
        out_specs=(VMEM, VMEM),
        scratch_shapes=[
            pltpu.VMEM((9, 1024, 256), BF),
            pltpu.VMEM((3, 1024, 1024), BF),
            pltpu.VMEM((3, 1024, 128), F32),
            pltpu.VMEM((288, 1024), BF),
            pltpu.VMEM((144, 1024), F32),
        ],
        name="sweep",
    )(tile_class, pack, points, area.reshape(1, 1024), connect, front_rows)
    core = lax.ppermute(node_part, ROW, [(i, i ^ 1) for i in range(4)])
    side = lax.ppermute(node_part, ROW, [(i, i ^ 2) for i in range(4)])
    cross = lax.ppermute(node_part, ROW, [(i, i ^ 3) for i in range(4)])
    front_sum = lax.all_to_all(front_part, COL, 0, 0)
    front_grad, node_grad = pl.pallas_call(
        last_kernel,
        out_shape=(shape((16, 48), F32), shape((48, 512), F32)),
        in_specs=[VMEM] * 5,
        out_specs=(VMEM, VMEM),
        name="last",
    )(front_sum, node_part, core, side, cross)
    return (front_grad, node_grad.T)


def solution(mesh):
    fine = Mesh(mesh.devices.reshape(2, 2, 8, 2, 4), ROW + COL)
    in_specs = (
        P(COL, ROW),
        P(COL, ROW),
        P(COL),
        P(None, COL),
        P(None, COL),
        P(ROW),
        P(ROW, COL),
    )
    out_specs = (P(ROW + COL, None), P(COL, None))
    return jax.shard_map(body, mesh=fine, in_specs=in_specs, out_specs=out_specs, check_vma=False)
```

```python
import jax
import jax.numpy as jnp
from jax import lax
from jax.experimental import pallas as pl
from jax.experimental.pallas import tpu as pltpu
from jax.sharding import Mesh, PartitionSpec as P

SOFTEN = 0.05
COL = ("z", "yh", "x")
ROW = ("yl", "co")
BF = jnp.bfloat16
F32 = jnp.float32

NT = (((1,), (1,)), ((), ()))
TN = (((0,), (0,)), ((), ()))


def iota(shape, dim):
    return lax.broadcasted_iota(jnp.int32, shape, dim)


def one_hot(mask):
    return jnp.where(mask, 1.0, 0.0).astype(BF)


CAP = 48
FAST = 1
SLOTS = 192


def ranks(owner):
    column = one_hot(iota((64, 1024), 0) == owner)
    group = one_hot(iota((16, 1024), 0) == (owner & 7))
    both = jnp.concatenate([column, group], 0)
    ahead = one_hot(iota((1024, 1024), 0) < iota((1024, 1024), 1))
    before = jnp.dot(both, ahead, preferred_element_type=F32) * both.astype(F32)
    inner = jnp.sum(before[:64], axis=0, keepdims=True).astype(jnp.int32)
    outer = jnp.sum(before[64:], axis=0, keepdims=True).astype(jnp.int32)
    return inner, outer


def take(slot, count, value):
    hit = jnp.where(iota((count, 1024), 0) == slot, value + 1.0, 0.0)
    return jnp.sum(hit, axis=1, keepdims=True) - 1.0


def prep_kernel(col_ref, gathered_ref, connect_ref, coords_ref, list_ref, pack_ref, points_ref, table_ref, pool_ref, place_ref, fits_ref):
    col = col_ref[0]
    place = iota((288, 320), 0)
    source = iota((288, 320), 1)
    group = place >> 4
    load = place & 15
    half = jnp.where(group >= 9, 1, 0)
    comp = group - 9 * half
    wanted = (load >> 2) * 80 + half * 36 + (load & 3) * 9 + comp
    permute = one_hot(source == wanted)
    gathered = gathered_ref[...].reshape(320, 1024)
    pack = jnp.dot(permute, gathered, preferred_element_type=F32).astype(BF)
    pack_ref[...] = pack
    base = jnp.concatenate([coords_ref[...].astype(F32), jnp.zeros((13, 512), F32)], 0)
    points = jnp.zeros((16, 1024), F32)
    for corner in range(3):
        chosen = one_hot(iota((512, 1024), 0) == connect_ref[corner : corner + 1, :] - col * 512)
        shifted = base if corner == 0 else pltpu.roll(base, 3 * corner, 0)
        points = points + jnp.dot(shifted.astype(BF), chosen, preferred_element_type=F32)
    points_ref[...] = points
    table = jnp.concatenate([pack[144:], pack[:144], points.astype(BF)], 0)
    table_ref[...] = table

    most = jnp.zeros((64, 1), F32)
    crowd = jnp.zeros((8, 1), F32)
    for r in range(4):
        owner = gathered[80 * r + 72 : 80 * r + 73, :].astype(jnp.int32) >> 2
        count = jnp.sum(jnp.where(iota((64, 1024), 0) == owner, 1.0, 0.0), axis=1, keepdims=True)
        most = jnp.maximum(most, count)
        crowd = jnp.maximum(crowd, jnp.sum(count.reshape(8, 8, 1), axis=0))
    fits = jnp.logical_and(jnp.max(most) <= CAP, jnp.max(crowd) <= SLOTS)
    fits_ref[0, 0] = jnp.where(fits, 1, 0).astype(jnp.int32)

    owner = list_ref[...] >> 10
    inner, outer = ranks(owner)
    place_ref[0:1, :] = (owner >> 3) * CAP + inner
    place_ref[1:2, :] = (owner & 7) * SLOTS + outer
    local = (list_ref[...] & 1023).astype(F32)
    slot = jnp.where(owner == col, inner, -1)
    chosen = take(slot, CAP, local).astype(jnp.int32)
    chosen = one_hot(iota((CAP, 1024), 1) == chosen)
    picked = lax.dot_general(chosen, table, NT, preferred_element_type=F32)
    picked = jnp.concatenate([picked, jnp.zeros((CAP, 80), F32)], 1)
    pool_ref[...] = jnp.broadcast_to(fold(picked, CAP).astype(BF)[None], pool_ref.shape)


def fold(rows, count):
    third = rows[:, 256:384]
    third = third[: count // 2] + pltpu.roll(third[count // 2 :], 64, 1)
    return jnp.concatenate([rows[:, 0:128], rows[:, 128:256], third], 0)


def unfold(pool, groups, count):
    half = count // 2
    third = pool[:, 2 * count :, :]
    turned = pltpu.roll(third.reshape(groups * half, 128), 64, 1).reshape(groups, half, 128)
    third = jnp.concatenate([third, turned], 1)
    blocks = [pool[:, 0:count, :], pool[:, count : 2 * count, :], third]
    return jnp.concatenate([block.reshape(groups * count, 128) for block in blocks], 1)


def merge_kernel(col_ref, pool_ref, place_ref, out_ref):
    mine = (col_ref[0] & 7) * SLOTS
    outer = place_ref[1:2, :] - mine
    chosen = take(outer, SLOTS, place_ref[0:1, :].astype(F32)).astype(jnp.int32)
    chosen = one_hot(iota((SLOTS, 8 * CAP), 1) == chosen)
    rows = unfold(pool_ref[...].astype(F32), 8, CAP).astype(BF)
    rows = jnp.dot(chosen, rows, preferred_element_type=F32)
    rows = jnp.where(iota((SLOTS, 384), 1) < 320, rows, 0.0)
    out_ref[...] = jnp.broadcast_to(fold(rows, SLOTS).astype(BF)[None], out_ref.shape)


def whole_kernel(col_ref, table_ref, list_ref, rows_ref):
    owned = one_hot(iota((1024, 1024), 0) == list_ref[...] - col_ref[0] * 1024)
    picked = jnp.dot(table_ref[...], owned, preferred_element_type=F32)
    picked = jnp.concatenate([picked, jnp.zeros((80, 1024), F32)], 0)
    rows_ref[...] = jnp.transpose(picked).astype(BF)


def main_kernel(
    col_ref,
    class_ref,
    pack_ref,
    points_ref,
    area_ref,
    connect_ref,
    pool_ref,
    slot_ref,
    front_ref,
    node_ref,
    kern_ref,
    dsum_ref,
    frontx_ref,
    fpack_ref,
    elem_ref,
):
    scale = (4096 * 65536) ** (-0.25) / 3.0
    weight = area_ref[...] * scale
    pool = unfold(pool_ref[...], 8, SLOTS)
    chosen = one_hot(iota((8 * SLOTS, 1024), 0) == slot_ref[1:2, :])
    found = lax.dot_general(pool, chosen, TN, preferred_element_type=F32)
    fpack_ref[...] = found[:288].astype(BF)
    tail = jnp.transpose(found[256:384])
    for k in range(3):
        value = (tail[:, 32 + k : 33 + k] + tail[:, 35 + k : 36 + k] + tail[:, 38 + k : 39 + k]) / 3.0
        frontx_ref[k] = jnp.broadcast_to(value, (1024, 128))
    points = [[points_ref[3 * a + k : 3 * a + k + 1, :] for k in range(3)] for a in range(3)]
    center = [(points[0][k] + points[1][k] + points[2][k]) / 3.0 for k in range(3)]

    for jt in range(4):
        cols = slice(256 * jt, 256 * jt + 256)
        wide = weight[:, cols]
        for it in range(4):
            vertex = class_ref[it, jt] == 1
            place = [
                [jnp.where(vertex, points[a][k][:, cols], center[k][:, cols]) for k in range(3)]
                for a in range(3)
            ]

            def chunk(step, carry):
                start = pl.multiple_of(256 * it + 16 * step, 16)
                at = pl.ds(start, 16)
                front = []
                for k in range(3):
                    piece = frontx_ref[k, at, :]
                    front.append(jnp.concatenate([piece, piece], 1))
                total = [None] * 3
                for a in range(3):
                    offset = [front[k] - place[a][k] for k in range(3)]
                    squared = (
                        offset[0] * offset[0] + offset[1] * offset[1] + offset[2] * offset[2] + SOFTEN
                    )
                    inverse = lax.rsqrt(squared)
                    factor = (wide * inverse) * (inverse * inverse)
                    for k in range(3):
                        value = offset[k] * factor
                        kern_ref[3 * a + k, at, :] = value.astype(BF)
                        total[k] = value if a == 0 else total[k] + value
                for k in range(3):
                    dsum_ref[k, at, cols] = total[k].astype(BF)
                return carry

            lax.fori_loop(0, 16, chunk, 0)
        leader = pack_ref[:, cols].astype(F32)
        for ak in range(9):
            product = jnp.dot(fpack_ref[...], kern_ref[ak], preferred_element_type=F32)
            joined = (product * leader).reshape(18, 16, 256)
            elem_ref[16 * ak : 16 * ak + 16, cols] = jnp.sum(joined, axis=0)

    pieces = []
    for k in range(3):
        product = lax.dot_general(pack_ref[...], dsum_ref[k], NT, preferred_element_type=F32)
        joined = (product * fpack_ref[...].astype(F32)).reshape(18, 16, 1024)
        pieces.append(-jnp.sum(joined, axis=0))
    pieces.append(jnp.zeros((80, 1024), F32))
    turned = jnp.transpose(jnp.concatenate(pieces, 0)).reshape(64, 16, 128)
    packed = turned[:, :8] + pltpu.roll(turned[:, 8:].reshape(512, 128), 64, 1).reshape(64, 8, 128)
    front_ref[...] = packed.astype(BF)

    nodes = jnp.zeros((96, 512), F32)
    for a in range(3):
        value = elem_ref[48 * a : 48 * a + 48, :]
        high = value.astype(BF)
        low = (value - high.astype(F32)).astype(BF)
        chosen = one_hot(iota((512, 1024), 0) == connect_ref[a : a + 1, :] - col_ref[0] * 512)
        nodes = nodes + lax.dot_general(
            jnp.concatenate([high, low], 0), chosen, NT, preferred_element_type=F32
        )
    node_ref[...] = (nodes[:48] + nodes[48:]).astype(BF)


def last_kernel(front_ref, own_ref, core_ref, side_ref, cross_ref, out_front_ref, out_node_ref):
    total = jnp.sum(front_ref[...].astype(F32), axis=0)
    out_front_ref[0:8, :] = total[:, 0:48]
    out_front_ref[8:16, :] = pltpu.roll(total, 64, 1)[:, 0:48]
    near = own_ref[...].astype(F32) + core_ref[...].astype(F32)
    far = side_ref[...].astype(F32) + cross_ref[...].astype(F32)
    out_node_ref[...] = near + far


def shape(dims, dtype):
    return jax.ShapeDtypeStruct(dims, dtype)


VMEM = pl.BlockSpec(memory_space=pltpu.VMEM)
SMEM = pl.BlockSpec(memory_space=pltpu.SMEM)


def body(state, adjoint, area, node_coords, connect, front_list, tile_class):
    col = lax.axis_index(COL).astype(jnp.int32).reshape(1)
    owners = (front_list >> 8).astype(BF).reshape(1, 1024)
    mine = jnp.concatenate([state.T, adjoint.T, owners, jnp.zeros((7, 1024), BF)], 0)
    gathered = lax.all_gather(mine, ROW)
    front_list = front_list.reshape(1, 1024)
    pack, points, table, pool, place, fits = pl.pallas_call(
        prep_kernel,
        out_shape=(
            shape((288, 1024), BF),
            shape((16, 1024), F32),
            shape((304, 1024), BF),
            shape((8, CAP * 5 // 2, 128), BF),
            shape((2, 1024), jnp.int32),
            shape((1, 1), jnp.int32),
        ),
        in_specs=[SMEM] + [VMEM] * 4,
        out_specs=(VMEM, VMEM, VMEM, VMEM, VMEM, SMEM),
        name="prep",
    )(col, gathered, connect, node_coords, front_list)

    def compact(pool, place, table):
        part = lax.all_to_all(pool, "z", 0, 0)
        merged = pl.pallas_call(
            merge_kernel,
            out_shape=shape((8, SLOTS * 5 // 2, 128), BF),
            in_specs=[SMEM] + [VMEM] * 2,
            out_specs=VMEM,
            name="merge",
        )(col, part, place)
        return lax.all_to_all(merged, ("yh", "x"), 0, 0), place

    def whole(pool, place, table):
        rows = pl.pallas_call(
            whole_kernel,
            out_shape=shape((1024, 384), BF),
            in_specs=[SMEM] + [VMEM] * 2,
            out_specs=VMEM,
            name="whole",
        )(col, table, front_list)
        part = lax.all_to_all(rows.reshape(64, 16, 384), COL, 0, 0)
        share = jnp.sum(part, axis=0, dtype=BF)
        spread = jnp.broadcast_to(share[None], (64, 16, 384))
        rows = lax.all_to_all(spread, COL, 0, 0).reshape(1024, 384)
        rows = jnp.pad(rows, ((0, 8 * SLOTS - 1024), (0, 0))).reshape(8, SLOTS, 384)
        third = rows[:, :, 256:320].reshape(8, 2, SLOTS // 2, 64)
        third = jnp.concatenate([third[:, 0], third[:, 1]], 2)
        pool = jnp.concatenate([rows[:, :, 0:128], rows[:, :, 128:256], third], 1)
        return pool, jnp.broadcast_to(jnp.arange(1024, dtype=jnp.int32), (2, 1024))

    fronts, slots = lax.cond(fits[0, 0] == FAST, compact, whole, pool, place, table)
    front_part, node_part = pl.pallas_call(
        main_kernel,
        out_shape=(shape((64, 8, 128), BF), shape((48, 512), BF)),
        in_specs=[SMEM] * 2 + [VMEM] * 6,
        out_specs=(VMEM, VMEM),
        scratch_shapes=[
            pltpu.VMEM((9, 1024, 256), BF),
            pltpu.VMEM((3, 1024, 1024), BF),
            pltpu.VMEM((3, 1024, 128), F32),
            pltpu.VMEM((288, 1024), BF),
            pltpu.VMEM((144, 1024), F32),
        ],
        name="sweep",
    )(col, tile_class, pack, points, area.reshape(1, 1024), connect, fronts, slots)
    core = lax.ppermute(node_part, ROW, [(i, i ^ 1) for i in range(4)])
    side = lax.ppermute(node_part, ROW, [(i, i ^ 2) for i in range(4)])
    cross = lax.ppermute(node_part, ROW, [(i, i ^ 3) for i in range(4)])
    front_sum = lax.all_to_all(front_part, COL, 0, 0)
    front_grad, node_grad = pl.pallas_call(
        last_kernel,
        out_shape=(shape((16, 48), F32), shape((48, 512), F32)),
        in_specs=[VMEM] * 5,
        out_specs=(VMEM, VMEM),
        name="last",
    )(front_sum, node_part, core, side, cross)
    return (front_grad, node_grad.T)


def solution(mesh):
    fine = Mesh(mesh.devices.reshape(2, 2, 8, 2, 4), ROW + COL)
    in_specs = (
        P(COL, ROW),
        P(COL, ROW),
        P(COL),
        P(None, COL),
        P(None, COL),
        P(ROW),
        P(ROW, COL),
    )
    out_specs = (P(ROW + COL, None), P(COL, None))
    return jax.shard_map(body, mesh=fine, in_specs=in_specs, out_specs=out_specs, check_vma=False)
```

```python
import jax
import jax.numpy as jnp
from jax import lax
from jax.experimental import pallas as pl
from jax.experimental.pallas import tpu as pltpu
from jax.sharding import Mesh, PartitionSpec as P

SOFTEN = 0.05
COL = ("z", "yh", "x")
ROW = ("yl", "co")
BF = jnp.bfloat16
F32 = jnp.float32

NT = (((1,), (1,)), ((), ()))
TN = (((0,), (0,)), ((), ()))


def iota(shape, dim):
    return lax.broadcasted_iota(jnp.int32, shape, dim)


def one_hot(mask):
    return jnp.where(mask, 1.0, 0.0).astype(BF)


CAP = 48
FAST = 1
SLOTS = 192


def ranks(owner):
    column = one_hot(iota((64, 1024), 0) == owner)
    group = one_hot(iota((16, 1024), 0) == (owner & 7))
    both = jnp.concatenate([column, group], 0)
    ahead = one_hot(iota((1024, 1024), 0) < iota((1024, 1024), 1))
    before = jnp.dot(both, ahead, preferred_element_type=F32) * both.astype(F32)
    inner = jnp.sum(before[:64], axis=0, keepdims=True).astype(jnp.int32)
    outer = jnp.sum(before[64:], axis=0, keepdims=True).astype(jnp.int32)
    return inner, outer


def take(slot, count, value):
    hit = jnp.where(iota((count, 1024), 0) == slot, value + 1.0, 0.0)
    return jnp.sum(hit, axis=1, keepdims=True) - 1.0


def prep_kernel(col_ref, gathered_ref, connect_ref, coords_ref, list_ref, pack_ref, points_ref, table_ref, pool_ref, place_ref, fits_ref):
    col = col_ref[0]
    place = iota((288, 320), 0)
    source = iota((288, 320), 1)
    group = place >> 4
    load = place & 15
    half = jnp.where(group >= 9, 1, 0)
    comp = group - 9 * half
    wanted = (load >> 2) * 80 + half * 36 + (load & 3) * 9 + comp
    permute = one_hot(source == wanted)
    gathered = gathered_ref[...].reshape(320, 1024)
    pack = jnp.dot(permute, gathered, preferred_element_type=F32).astype(BF)
    pack_ref[...] = pack
    base = jnp.concatenate([coords_ref[...].astype(F32), jnp.zeros((13, 512), F32)], 0)
    points = jnp.zeros((16, 1024), F32)
    for corner in range(3):
        chosen = one_hot(iota((512, 1024), 0) == connect_ref[corner : corner + 1, :] - col * 512)
        shifted = base if corner == 0 else pltpu.roll(base, 3 * corner, 0)
        points = points + jnp.dot(shifted.astype(BF), chosen, preferred_element_type=F32)
    points_ref[...] = points
    table = jnp.concatenate([pack[144:], pack[:144], points.astype(BF)], 0)
    table_ref[...] = table

    most = jnp.zeros((64, 1), F32)
    crowd = jnp.zeros((8, 1), F32)
    for r in range(4):
        owner = gathered[80 * r + 72 : 80 * r + 73, :].astype(jnp.int32) >> 2
        count = jnp.sum(jnp.where(iota((64, 1024), 0) == owner, 1.0, 0.0), axis=1, keepdims=True)
        most = jnp.maximum(most, count)
        crowd = jnp.maximum(crowd, jnp.sum(count.reshape(8, 8, 1), axis=0))
    fits = jnp.logical_and(jnp.max(most) <= CAP, jnp.max(crowd) <= SLOTS)
    fits_ref[0, 0] = jnp.where(fits, 1, 0).astype(jnp.int32)

    owner = list_ref[...] >> 10
    inner, outer = ranks(owner)
    place_ref[0:1, :] = (owner >> 3) * CAP + inner
    place_ref[1:2, :] = (owner & 7) * SLOTS + outer
    local = (list_ref[...] & 1023).astype(F32)
    slot = jnp.where(owner == col, inner, -1)
    chosen = take(slot, CAP, local).astype(jnp.int32)
    chosen = one_hot(iota((CAP, 1024), 1) == chosen)
    picked = lax.dot_general(chosen, table, NT, preferred_element_type=F32)
    picked = jnp.concatenate([picked, jnp.zeros((CAP, 80), F32)], 1)
    pool_ref[...] = jnp.broadcast_to(fold(picked, CAP).astype(BF)[None], pool_ref.shape)


def fold(rows, count):
    third = rows[:, 256:384]
    third = third[: count // 2] + pltpu.roll(third[count // 2 :], 64, 1)
    return jnp.concatenate([rows[:, 0:128], rows[:, 128:256], third], 0)


def unfold(pool, groups, count):
    half = count // 2
    third = pool[:, 2 * count :, :]
    turned = pltpu.roll(third.reshape(groups * half, 128), 64, 1).reshape(groups, half, 128)
    third = jnp.concatenate([third, turned], 1)
    blocks = [pool[:, 0:count, :], pool[:, count : 2 * count, :], third]
    return jnp.concatenate([block.reshape(groups * count, 128) for block in blocks], 1)


def merge_kernel(col_ref, pool_ref, place_ref, out_ref):
    mine = (col_ref[0] & 7) * SLOTS
    outer = place_ref[1:2, :] - mine
    chosen = take(outer, SLOTS, place_ref[0:1, :].astype(F32)).astype(jnp.int32)
    chosen = one_hot(iota((SLOTS, 8 * CAP), 1) == chosen)
    rows = unfold(pool_ref[...].astype(F32), 8, CAP).astype(BF)
    rows = jnp.dot(chosen, rows, preferred_element_type=F32)
    rows = jnp.where(iota((SLOTS, 384), 1) < 320, rows, 0.0)
    out_ref[...] = jnp.broadcast_to(fold(rows, SLOTS).astype(BF)[None], out_ref.shape)


def whole_kernel(col_ref, table_ref, list_ref, rows_ref):
    owned = one_hot(iota((1024, 1024), 0) == list_ref[...] - col_ref[0] * 1024)
    picked = jnp.dot(table_ref[...], owned, preferred_element_type=F32)
    picked = jnp.concatenate([picked, jnp.zeros((80, 1024), F32)], 0)
    rows_ref[...] = jnp.transpose(picked).astype(BF)


def load_sum(product, count):
    return jnp.sum(product.reshape(18, 16, count), axis=0)


def main_kernel(
    col_ref,
    class_ref,
    pack_ref,
    points_ref,
    area_ref,
    connect_ref,
    coords_ref,
    pool_ref,
    slot_ref,
    front_ref,
    node_ref,
    knode_ref,
    kcell_ref,
    frontx_ref,
    fpack_ref,
    share_ref,
    touch_ref,
    part_ref,
    nsum_ref,
    nhalf_ref,
    elem_ref,
):
    scale = (4096 * 65536) ** (-0.25) / 3.0
    weight = area_ref[...] * scale
    pool = unfold(pool_ref[...], 8, SLOTS)
    chosen = one_hot(iota((8 * SLOTS, 1024), 0) == slot_ref[1:2, :])
    found = lax.dot_general(pool, chosen, TN, preferred_element_type=F32)
    fpack_ref[...] = found[:288].astype(BF)
    tail = jnp.transpose(found[256:384])
    for k in range(3):
        value = (tail[:, 32 + k : 33 + k] + tail[:, 35 + k : 36 + k] + tail[:, 38 + k : 39 + k]) / 3.0
        frontx_ref[k] = jnp.broadcast_to(value, (1024, 128))
    rows = [[points_ref[3 * a + k : 3 * a + k + 1, :] for k in range(3)] for a in range(3)]
    center = [(rows[0][k] + rows[1][k] + rows[2][k]) / 3.0 for k in range(3)]
    corner = [coords_ref[k : k + 1, :].astype(F32) for k in range(3)]

    def fill(out_ref, place, first, count, lanes):
        width = place[0].shape[1]
        place = [jnp.broadcast_to(p, (16, width)) for p in place]

        def chunk(step, carry):
            at = pl.ds(pl.multiple_of(first + 16 * step, 16), 16)
            offset = []
            for k in range(3):
                piece = frontx_ref[k, at, :]
                offset.append(jnp.concatenate([piece] * (width // 128), 1) - place[k])
            squared = offset[0] * offset[0] + offset[1] * offset[1] + offset[2] * offset[2] + SOFTEN
            inverse = lax.rsqrt(squared)
            factor = inverse * inverse * inverse
            for k in range(3):
                out_ref[k, at, lanes] = (offset[k] * factor).astype(BF)
            return carry

        lax.fori_loop(0, count // 16, chunk, 0, unroll=4)

    for half in range(2):
        lanes = slice(256 * half, 256 * half + 256)
        fill(knode_ref, [c[:, lanes] for c in corner], 0, 1024, lanes)
    for jt in range(4):
        lanes = slice(256 * jt, 256 * jt + 256)
        place = [c[:, lanes] for c in center]
        for it in range(4):
            vertex = class_ref[it, jt] == 1

            @pl.when(vertex)
            def _():
                kcell_ref[:, 256 * it : 256 * it + 256, lanes] = jnp.zeros((3, 256, 256), BF)

            @pl.when(jnp.logical_not(vertex))
            def _():
                fill(kcell_ref, place, 256 * it, 256, lanes)

    share_ref[...] = (pack_ref[...].astype(F32) * weight).astype(BF)
    ends = [jnp.broadcast_to(connect_ref[a : a + 1, :] - col_ref[0] * 512, (16, 1024)) for a in range(3)]

    def mark(step, carry):
        at = pl.multiple_of(16 * step, 16)
        node = iota((16, 1024), 0) + at
        hit = (node == ends[0]) | (node == ends[1]) | (node == ends[2])
        touch_ref[pl.ds(at, 16), :] = one_hot(hit)
        return carry

    lax.fori_loop(0, 32, mark, 0, unroll=2)
    for jt in range(4):
        lanes = slice(256 * jt, 256 * jt + 256)
        part_ref[jt] = lax.dot_general(
            share_ref[:, lanes], touch_ref[:, lanes], NT, preferred_element_type=F32
        )
    mask = [[class_ref[it, jt].astype(F32) for jt in range(4)] for it in range(4)]

    def blend(step, carry):
        at = pl.ds(pl.multiple_of(16 * step, 16), 16)
        part = [part_ref[jt, at, :] for jt in range(4)]
        for it in range(4):
            total = part[0] * mask[it][0]
            for jt in range(1, 4):
                total = total + part[jt] * mask[it][jt]
            nsum_ref[it, at, :] = total
            nhalf_ref[it, at, :] = total.astype(BF)
        return carry

    lax.fori_loop(0, 18, blend, 0)

    for jt in range(4):
        lanes = slice(256 * jt, 256 * jt + 256)
        leader = pack_ref[:, lanes].astype(F32) * weight[:, lanes]
        for k in range(3):
            product = jnp.dot(fpack_ref[...], kcell_ref[k, :, lanes], preferred_element_type=F32)
            elem_ref[16 * k : 16 * k + 16, lanes] = load_sum(product * leader, 256)

    nodes = []
    for k in range(3):
        total = None
        for it in range(4):
            rows = slice(256 * it, 256 * it + 256)
            product = jnp.dot(fpack_ref[:, rows], knode_ref[k, rows, :], preferred_element_type=F32)
            value = load_sum(product * nsum_ref[it], 512)
            total = value if it == 0 else total + value
        nodes.append(total)
    value = elem_ref[...]
    high = value.astype(BF)
    low = (value - high.astype(F32)).astype(BF)
    spread = lax.dot_general(
        jnp.concatenate([high, low], 0), touch_ref[...], NT, preferred_element_type=F32
    )
    node_ref[...] = (jnp.concatenate(nodes, 0) + (spread[:48] + spread[48:])).astype(BF)

    columns = []
    for it in range(4):
        rows = slice(256 * it, 256 * it + 256)
        leader = fpack_ref[:, rows].astype(F32)
        pieces = []
        for k in range(3):
            product = 3.0 * lax.dot_general(
                share_ref[...], kcell_ref[k, rows, :], NT, preferred_element_type=F32
            ) + lax.dot_general(
                nhalf_ref[it], knode_ref[k, rows, :], NT, preferred_element_type=F32
            )
            pieces.append(-load_sum(product * leader, 256))
        pieces.append(jnp.zeros((80, 256), F32))
        columns.append(jnp.transpose(jnp.concatenate(pieces, 0)))
    turned = jnp.concatenate(columns, 0).reshape(64, 16, 128)
    packed = turned[:, :8] + pltpu.roll(turned[:, 8:].reshape(512, 128), 64, 1).reshape(64, 8, 128)
    front_ref[...] = packed.astype(BF)


def last_kernel(front_ref, own_ref, core_ref, side_ref, cross_ref, out_front_ref, out_node_ref):
    total = jnp.sum(front_ref[...].astype(F32), axis=0)
    out_front_ref[0:8, :] = total[:, 0:48]
    out_front_ref[8:16, :] = pltpu.roll(total, 64, 1)[:, 0:48]
    near = own_ref[...].astype(F32) + core_ref[...].astype(F32)
    far = side_ref[...].astype(F32) + cross_ref[...].astype(F32)
    out_node_ref[...] = near + far


def shape(dims, dtype):
    return jax.ShapeDtypeStruct(dims, dtype)


VMEM = pl.BlockSpec(memory_space=pltpu.VMEM)
SMEM = pl.BlockSpec(memory_space=pltpu.SMEM)


def body(state, adjoint, area, node_coords, connect, front_list, tile_class):
    col = lax.axis_index(COL).astype(jnp.int32).reshape(1)
    owners = (front_list >> 8).astype(BF).reshape(1, 1024)
    mine = jnp.concatenate([state.T, adjoint.T, owners, jnp.zeros((7, 1024), BF)], 0)
    gathered = lax.all_gather(mine, ROW)
    front_list = front_list.reshape(1, 1024)
    pack, points, table, pool, place, fits = pl.pallas_call(
        prep_kernel,
        out_shape=(
            shape((288, 1024), BF),
            shape((16, 1024), F32),
            shape((304, 1024), BF),
            shape((8, CAP * 5 // 2, 128), BF),
            shape((2, 1024), jnp.int32),
            shape((1, 1), jnp.int32),
        ),
        in_specs=[SMEM] + [VMEM] * 4,
        out_specs=(VMEM, VMEM, VMEM, VMEM, VMEM, SMEM),
        compiler_params=pltpu.CompilerParams(vmem_limit_bytes=24 << 20),
        name="prep",
    )(col, gathered, connect, node_coords, front_list)

    def compact(pool, place, table):
        part = lax.all_to_all(pool, "z", 0, 0)
        merged = pl.pallas_call(
            merge_kernel,
            out_shape=shape((8, SLOTS * 5 // 2, 128), BF),
            in_specs=[SMEM] + [VMEM] * 2,
            out_specs=VMEM,
            compiler_params=pltpu.CompilerParams(vmem_limit_bytes=24 << 20),
            name="merge",
        )(col, part, place)
        return lax.all_to_all(merged, ("yh", "x"), 0, 0), place

    def whole(pool, place, table):
        rows = pl.pallas_call(
            whole_kernel,
            out_shape=shape((1024, 384), BF),
            in_specs=[SMEM] + [VMEM] * 2,
            out_specs=VMEM,
            name="whole",
        )(col, table, front_list)
        part = lax.all_to_all(rows.reshape(64, 16, 384), COL, 0, 0)
        share = jnp.sum(part, axis=0, dtype=BF)
        spread = jnp.broadcast_to(share[None], (64, 16, 384))
        rows = lax.all_to_all(spread, COL, 0, 0).reshape(1024, 384)
        rows = jnp.pad(rows, ((0, 8 * SLOTS - 1024), (0, 0))).reshape(8, SLOTS, 384)
        third = rows[:, :, 256:320].reshape(8, 2, SLOTS // 2, 64)
        third = jnp.concatenate([third[:, 0], third[:, 1]], 2)
        pool = jnp.concatenate([rows[:, :, 0:128], rows[:, :, 128:256], third], 1)
        return pool, jnp.broadcast_to(jnp.arange(1024, dtype=jnp.int32), (2, 1024))

    fronts, slots = lax.cond(fits[0, 0] == FAST, compact, whole, pool, place, table)
    front_part, node_part = pl.pallas_call(
        main_kernel,
        out_shape=(shape((64, 8, 128), BF), shape((48, 512), BF)),
        in_specs=[SMEM] * 2 + [VMEM] * 7,
        out_specs=(VMEM, VMEM),
        scratch_shapes=[
            pltpu.VMEM((3, 1024, 512), BF),
            pltpu.VMEM((3, 1024, 1024), BF),
            pltpu.VMEM((3, 1024, 128), F32),
            pltpu.VMEM((288, 1024), BF),
            pltpu.VMEM((288, 1024), BF),
            pltpu.VMEM((512, 1024), BF),
            pltpu.VMEM((4, 288, 512), F32),
            pltpu.VMEM((4, 288, 512), F32),
            pltpu.VMEM((4, 288, 512), BF),
            pltpu.VMEM((48, 1024), F32),
        ],
        compiler_params=pltpu.CompilerParams(vmem_limit_bytes=44 << 20),
        name="sweep",
    )(
        col,
        tile_class,
        pack,
        points,
        area.reshape(1, 1024),
        connect,
        node_coords,
        fronts,
        slots,
    )
    core = lax.ppermute(node_part, ROW, [(i, i ^ 1) for i in range(4)])
    side = lax.ppermute(node_part, ROW, [(i, i ^ 2) for i in range(4)])
    cross = lax.ppermute(node_part, ROW, [(i, i ^ 3) for i in range(4)])
    front_sum = lax.all_to_all(front_part, COL, 0, 0)
    front_grad, node_grad = pl.pallas_call(
        last_kernel,
        out_shape=(shape((16, 48), F32), shape((48, 512), F32)),
        in_specs=[VMEM] * 5,
        out_specs=(VMEM, VMEM),
        compiler_params=pltpu.CompilerParams(vmem_limit_bytes=16 << 20),
        name="last",
    )(front_sum, node_part, core, side, cross)
    return (front_grad, node_grad.T)


def solution(mesh):
    fine = Mesh(mesh.devices.reshape(2, 2, 8, 2, 4), ROW + COL)
    in_specs = (
        P(COL, ROW),
        P(COL, ROW),
        P(COL),
        P(None, COL),
        P(None, COL),
        P(ROW),
        P(ROW, COL),
    )
    out_specs = (P(ROW + COL, None), P(COL, None))
    return jax.shard_map(body, mesh=fine, in_specs=in_specs, out_specs=out_specs, check_vma=False)
```

```python
import jax
import jax.numpy as jnp
from jax import lax
from jax.experimental import pallas as pl
from jax.experimental.pallas import tpu as pltpu
from jax.sharding import Mesh, PartitionSpec as P

SOFTEN = 0.05
COL = ("z", "yh", "x")
ROW = ("yl", "co")
BF = jnp.bfloat16
F32 = jnp.float32

NT = (((1,), (1,)), ((), ()))
TN = (((0,), (0,)), ((), ()))


def iota(shape, dim):
    return lax.broadcasted_iota(jnp.int32, shape, dim)


def one_hot(mask):
    return jnp.where(mask, 1.0, 0.0).astype(BF)


CAP = 40
CAP_HALF = 24
FAST = 1
SLOTS = 176
SLOT_HALF = 96


def ranks(owner):
    column = one_hot(iota((64, 1024), 0) == owner)
    group = one_hot(iota((16, 1024), 0) == (owner & 7))
    both = jnp.concatenate([column, group], 0)
    ahead = one_hot(iota((1024, 1024), 0) < iota((1024, 1024), 1))
    before = jnp.dot(both, ahead, preferred_element_type=F32) * both.astype(F32)
    inner = jnp.sum(before[:64], axis=0, keepdims=True).astype(jnp.int32)
    outer = jnp.sum(before[64:], axis=0, keepdims=True).astype(jnp.int32)
    return inner, outer


def take(slot, count, value):
    hit = jnp.where(iota((count, 1024), 0) == slot, value + 1.0, 0.0)
    return jnp.sum(hit, axis=1, keepdims=True) - 1.0


def prep_kernel(col_ref, gathered_ref, connect_ref, coords_ref, list_ref, pack_ref, points_ref, table_ref, pool_ref, place_ref, fits_ref):
    col = col_ref[0]
    place = iota((288, 320), 0)
    source = iota((288, 320), 1)
    group = place >> 4
    load = place & 15
    half = jnp.where(group >= 9, 1, 0)
    comp = group - 9 * half
    wanted = (load >> 2) * 80 + half * 36 + (load & 3) * 9 + comp
    permute = one_hot(source == wanted)
    gathered = gathered_ref[...].reshape(320, 1024)
    pack = jnp.dot(permute, gathered, preferred_element_type=F32).astype(BF)
    pack_ref[...] = pack
    base = jnp.concatenate([coords_ref[...].astype(F32), jnp.zeros((13, 512), F32)], 0)
    points = jnp.zeros((16, 1024), F32)
    for corner in range(3):
        chosen = one_hot(iota((512, 1024), 0) == connect_ref[corner : corner + 1, :] - col * 512)
        shifted = base if corner == 0 else pltpu.roll(base, 3 * corner, 0)
        points = points + jnp.dot(shifted.astype(BF), chosen, preferred_element_type=F32)
    points_ref[...] = points
    table = jnp.concatenate([pack[144:], pack[:144], points.astype(BF)], 0)
    table_ref[...] = table

    most = jnp.zeros((64, 1), F32)
    crowd = jnp.zeros((8, 1), F32)
    for r in range(4):
        owner = gathered[80 * r + 72 : 80 * r + 73, :].astype(jnp.int32) >> 2
        count = jnp.sum(jnp.where(iota((64, 1024), 0) == owner, 1.0, 0.0), axis=1, keepdims=True)
        most = jnp.maximum(most, count)
        crowd = jnp.maximum(crowd, jnp.sum(count.reshape(8, 8, 1), axis=0))
    fits = jnp.logical_and(jnp.max(most) <= CAP, jnp.max(crowd) <= SLOTS)
    fits_ref[0, 0] = jnp.where(fits, 1, 0).astype(jnp.int32)

    owner = list_ref[...] >> 10
    inner, outer = ranks(owner)
    place_ref[0:1, :] = (owner >> 3) * CAP + inner
    place_ref[1:2, :] = (owner & 7) * SLOTS + outer
    local = (list_ref[...] & 1023).astype(F32)
    slot = jnp.where(owner == col, inner, -1)
    chosen = take(slot, CAP, local).astype(jnp.int32)
    chosen = one_hot(iota((CAP, 1024), 1) == chosen)
    picked = lax.dot_general(chosen, table, NT, preferred_element_type=F32)
    picked = jnp.concatenate([picked, jnp.zeros((CAP, 80), F32)], 1)
    pool_ref[...] = jnp.broadcast_to(fold(picked, CAP, CAP_HALF).astype(BF)[None], pool_ref.shape)


def fold(rows, count, half):
    third = rows[:, 256:384]
    turned = pltpu.roll(third[half:], 64, 1)
    turned = jnp.concatenate([turned, jnp.zeros((2 * half - count, 128), F32)], 0)
    return jnp.concatenate([rows[:, 0:128], rows[:, 128:256], third[:half] + turned], 0)


def unfold(pool, groups, count, half):
    third = pool[:, 2 * count :, :]
    turned = pltpu.roll(third.reshape(groups * half, 128), 64, 1).reshape(groups, half, 128)
    third = jnp.concatenate([third, turned[:, : count - half]], 1)
    blocks = [pool[:, 0:count, :], pool[:, count : 2 * count, :], third]
    return jnp.concatenate([block.reshape(groups * count, 128) for block in blocks], 1)


def merge_kernel(col_ref, pool_ref, place_ref, out_ref):
    mine = (col_ref[0] & 7) * SLOTS
    outer = place_ref[1:2, :] - mine
    chosen = take(outer, SLOTS, place_ref[0:1, :].astype(F32)).astype(jnp.int32)
    chosen = one_hot(iota((SLOTS, 8 * CAP), 1) == chosen)
    rows = unfold(pool_ref[...].astype(F32), 8, CAP, CAP_HALF).astype(BF)
    rows = jnp.dot(chosen, rows, preferred_element_type=F32)
    rows = jnp.where(iota((SLOTS, 384), 1) < 320, rows, 0.0)
    out_ref[...] = jnp.broadcast_to(fold(rows, SLOTS, SLOT_HALF).astype(BF)[None], out_ref.shape)


def join_kernel(state_ref, adjoint_ref, list_ref, out_ref, left_ref, right_ref, row_ref, sems):
    copies = [
        pltpu.make_async_copy(state_ref, left_ref, sems.at[0]),
        pltpu.make_async_copy(adjoint_ref, right_ref, sems.at[1]),
        pltpu.make_async_copy(list_ref, row_ref, sems.at[2]),
    ]
    for copy in copies:
        copy.start()
    for copy in copies:
        copy.wait()
    owner = (row_ref[...] >> 8).astype(F32)
    pieces = [left_ref[...].astype(F32), right_ref[...].astype(F32), owner, jnp.zeros((7, 1024), F32)]
    out_ref[...] = jnp.concatenate(pieces, 0).astype(BF)


def whole_kernel(col_ref, table_ref, list_ref, rows_ref):
    owned = one_hot(iota((1024, 1024), 0) == list_ref[...] - col_ref[0] * 1024)
    picked = jnp.dot(table_ref[...], owned, preferred_element_type=F32)
    picked = jnp.concatenate([picked, jnp.zeros((80, 1024), F32)], 0)
    rows_ref[...] = jnp.transpose(picked).astype(BF)


def load_sum(product, count):
    return jnp.sum(product.reshape(18, 16, count), axis=0)


def main_kernel(
    col_ref,
    class_ref,
    pack_ref,
    points_ref,
    area_ref,
    connect_ref,
    coords_ref,
    pool_ref,
    slot_ref,
    front_ref,
    node_ref,
    knode_ref,
    kcell_ref,
    frontx_ref,
    fpack_ref,
    share_ref,
    touch_ref,
    part_ref,
    nsum_ref,
    nhalf_ref,
    elem_ref,
    place_ref,
):
    scale = (4096 * 65536) ** (-0.25) / 3.0
    weight = area_ref[...] * scale
    pool = jnp.transpose(unfold(pool_ref[...], 8, SLOTS, SLOT_HALF))[:304]
    chosen = one_hot(iota((8 * SLOTS, 1024), 0) == slot_ref[1:2, :])
    found = jnp.dot(pool, chosen, preferred_element_type=F32)
    fpack_ref[...] = found[:288].astype(BF)
    tail = found[288:304]
    tail = [(tail[k : k + 1] + tail[3 + k : 4 + k] + tail[6 + k : 7 + k]) / 3.0 for k in range(3)]
    tail = jnp.transpose(jnp.concatenate(tail + [jnp.zeros((5, 1024), F32)], 0))
    for k in range(3):
        frontx_ref[k] = jnp.broadcast_to(tail[:, k : k + 1], (1024, 128))
    rows = [[points_ref[3 * a + k : 3 * a + k + 1, :] for k in range(3)] for a in range(3)]
    center = [(rows[0][k] + rows[1][k] + rows[2][k]) / 3.0 for k in range(3)]
    corner = [coords_ref[k : k + 1, :].astype(F32) for k in range(3)]

    mask = [[class_ref[it, jt].astype(F32) for jt in range(4)] for it in range(4)]

    for k in range(3):
        place_ref[k, :, 0:512] = jnp.broadcast_to(corner[k], (8, 512))
        place_ref[k, :, 512:1536] = jnp.broadcast_to(center[k], (8, 1024))

    def fill(out_ref, step, lanes, shift, soften):
        at = slice(16 * step, 16 * step + 16)
        offset = []
        for k in range(3):
            piece = frontx_ref[k, at, :]
            place = place_ref[k, :, lanes.start + shift : lanes.stop + shift]
            place = jnp.concatenate([place, place], 0)
            offset.append(jnp.concatenate([piece, piece], 1) - place)
        squared = offset[0] * offset[0] + offset[1] * offset[1] + offset[2] * offset[2] + soften
        inverse = lax.rsqrt(squared)
        factor = inverse * inverse * inverse
        for k in range(3):
            out_ref[k, at, lanes] = (offset[k] * factor).astype(BF)

    def weave(many, few):
        done = 0
        for place, job in enumerate(many):
            while done < len(few) and done * len(many) <= place * len(few):
                few[done]()
                done += 1
            job()
        for job in few[done:]:
            job()

    share_ref[...] = (pack_ref[...].astype(F32) * weight).astype(BF)
    ends = [jnp.broadcast_to(connect_ref[a : a + 1, :] - col_ref[0] * 512, (16, 1024)) for a in range(3)]

    def mark(step):
        node = iota((16, 1024), 0) + 16 * step
        hit = (node == ends[0]) | (node == ends[1]) | (node == ends[2])
        touch_ref[16 * step : 16 * step + 16, :] = one_hot(hit)

    for step in range(32):
        mark(step)

    def part(jt):
        lanes = slice(256 * jt, 256 * jt + 256)
        part_ref[jt] = lax.dot_general(
            share_ref[:, lanes], touch_ref[:, lanes], NT, preferred_element_type=F32
        )

    def node_fill(step, half):
        fill(knode_ref, step, slice(256 * half, 256 * half + 256), 0, SOFTEN)

    def cell_fill(step, jt):
        soften = jnp.where(class_ref[step // 16, jt] == 1, 3.0e38, SOFTEN).astype(F32)
        fill(kcell_ref, step, slice(256 * jt, 256 * jt + 256), 512, soften)

    weave(
        [lambda s=s, h=h: node_fill(s, h) for h in range(2) for s in range(64)],
        [lambda jt=jt: part(jt) for jt in range(4)],
    )

    def blend(step):
        at = slice(16 * step, 16 * step + 16)
        part = [part_ref[jt, at, :] for jt in range(4)]
        for it in range(4):
            total = part[0] * mask[it][0]
            for jt in range(1, 4):
                total = total + part[jt] * mask[it][jt]
            nsum_ref[it, at, :] = total
            nhalf_ref[it, at, :] = total.astype(BF)

    nodes = [[], [], []]

    def node_dot(k, it):
        rows = slice(256 * it, 256 * it + 256)
        product = jnp.dot(fpack_ref[:, rows], knode_ref[k, rows, :], preferred_element_type=F32)
        nodes[k].append(load_sum(product * nsum_ref[it], 512))

    def cell_dot(k, jt):
        lanes = slice(256 * jt, 256 * jt + 256)
        leader = pack_ref[:, lanes].astype(F32) * weight[:, lanes]
        product = jnp.dot(fpack_ref[...], kcell_ref[k, :, lanes], preferred_element_type=F32)
        elem_ref[16 * k : 16 * k + 16, lanes] = load_sum(product * leader, 256)

    weave(
        [lambda s=s, jt=jt: cell_fill(s, jt) for jt in range(2) for s in range(64)],
        [lambda s=s: blend(s) for s in range(18)]
        + [lambda k=k, it=it: node_dot(k, it) for k in range(3) for it in range(4)]
        + [lambda k=k: cell_dot(k, 0) for k in range(3)],
    )

    pieces = [[] for it in range(4)]

    def row_dot(k, it):
        rows = slice(256 * it, 256 * it + 256)
        product = 3.0 * lax.dot_general(
            share_ref[...], kcell_ref[k, rows, :], NT, preferred_element_type=F32
        ) + lax.dot_general(nhalf_ref[it], knode_ref[k, rows, :], NT, preferred_element_type=F32)
        pieces[it].append(-load_sum(product * fpack_ref[:, rows].astype(F32), 256))

    for it in range(4):
        if it == 0:
            few = [lambda k=k: cell_dot(k, 1) for k in range(3)]
        else:
            few = [lambda k=k, it=it: row_dot(k, it - 1) for k in range(3)]
        weave([lambda s=s, jt=jt, it=it: cell_fill(16 * it + s, jt) for s in range(16) for jt in (2, 3)], few)
    for k in range(3):
        row_dot(k, 3)
    for jt in (2, 3):
        for k in range(3):
            cell_dot(k, jt)
    nodes = jnp.concatenate([part[0] + part[1] + part[2] + part[3] for part in nodes], 0)
    value = elem_ref[...]
    high = value.astype(BF)
    low = (value - high.astype(F32)).astype(BF)
    spread = lax.dot_general(
        jnp.concatenate([high, low], 0), touch_ref[...], NT, preferred_element_type=F32
    )
    node_ref[...] = (nodes + (spread[:48] + spread[48:])).astype(BF)

    columns = []
    for it in range(4):
        filled = jnp.concatenate(pieces[it] + [jnp.zeros((80, 256), F32)], 0)
        columns.append(jnp.transpose(filled))
    turned = jnp.concatenate(columns, 0).reshape(64, 16, 128)
    packed = turned[:, :8] + pltpu.roll(turned[:, 8:].reshape(512, 128), 64, 1).reshape(64, 8, 128)
    front_ref[...] = packed.astype(BF)


def last_kernel(front_ref, own_ref, core_ref, side_ref, cross_ref, out_front_ref, out_node_ref):
    total = jnp.sum(front_ref[...].astype(F32), axis=0)
    out_front_ref[0:8, :] = total[:, 0:48]
    out_front_ref[8:16, :] = pltpu.roll(total, 64, 1)[:, 0:48]
    near = own_ref[...].astype(F32) + core_ref[...].astype(F32)
    far = side_ref[...].astype(F32) + cross_ref[...].astype(F32)
    out_node_ref[...] = near + far


def shape(dims, dtype):
    return jax.ShapeDtypeStruct(dims, dtype)


VMEM = pl.BlockSpec(memory_space=pltpu.VMEM)
HBM = pl.BlockSpec(memory_space=pltpu.HBM)
SMEM = pl.BlockSpec(memory_space=pltpu.SMEM)


def body(state, adjoint, area, node_coords, connect, front_list, tile_class):
    col = lax.axis_index(COL).astype(jnp.int32).reshape(1)
    front_list = front_list.reshape(1, 1024)
    mine = pl.pallas_call(
        join_kernel,
        out_shape=shape((80, 1024), BF),
        in_specs=[HBM] * 3,
        out_specs=VMEM,
        scratch_shapes=[
            pltpu.VMEM((36, 1024), BF),
            pltpu.VMEM((36, 1024), BF),
            pltpu.VMEM((1, 1024), jnp.int32),
            pltpu.SemaphoreType.DMA((3,)),
        ],
        name="join",
    )(state.T, adjoint.T, front_list)
    gathered = lax.all_gather(mine, ROW)
    pack, points, table, pool, place, fits = pl.pallas_call(
        prep_kernel,
        out_shape=(
            shape((288, 1024), BF),
            shape((16, 1024), F32),
            shape((304, 1024), BF),
            shape((8, 2 * CAP + CAP_HALF, 128), BF),
            shape((2, 1024), jnp.int32),
            shape((1, 1), jnp.int32),
        ),
        in_specs=[SMEM] + [VMEM] * 4,
        out_specs=(VMEM, VMEM, VMEM, VMEM, VMEM, SMEM),
        compiler_params=pltpu.CompilerParams(vmem_limit_bytes=24 << 20),
        name="prep",
    )(col, gathered, connect, node_coords, front_list)

    def compact(pool, place, table):
        part = lax.all_to_all(pool, "z", 0, 0)
        merged = pl.pallas_call(
            merge_kernel,
            out_shape=shape((8, 2 * SLOTS + SLOT_HALF, 128), BF),
            in_specs=[SMEM] + [VMEM] * 2,
            out_specs=VMEM,
            compiler_params=pltpu.CompilerParams(vmem_limit_bytes=24 << 20),
            name="merge",
        )(col, part, place)
        return lax.all_to_all(merged, ("yh", "x"), 0, 0), place

    def whole(pool, place, table):
        rows = pl.pallas_call(
            whole_kernel,
            out_shape=shape((1024, 384), BF),
            in_specs=[SMEM] + [VMEM] * 2,
            out_specs=VMEM,
            name="whole",
        )(col, table, front_list)
        part = lax.all_to_all(rows.reshape(64, 16, 384), COL, 0, 0)
        share = jnp.sum(part, axis=0, dtype=BF)
        spread = jnp.broadcast_to(share[None], (64, 16, 384))
        rows = lax.all_to_all(spread, COL, 0, 0).reshape(1024, 384)
        rows = jnp.pad(rows, ((0, 8 * SLOTS - 1024), (0, 0))).reshape(8, SLOTS, 384)
        third = jnp.pad(rows[:, :, 256:320], ((0, 0), (0, 2 * SLOT_HALF - SLOTS), (0, 0)))
        third = jnp.concatenate([third[:, :SLOT_HALF], third[:, SLOT_HALF:]], 2)
        pool = jnp.concatenate([rows[:, :, 0:128], rows[:, :, 128:256], third], 1)
        return pool, jnp.broadcast_to(jnp.arange(1024, dtype=jnp.int32), (2, 1024))

    fronts, slots = lax.cond(fits[0, 0] == FAST, compact, whole, pool, place, table)
    front_part, node_part = pl.pallas_call(
        main_kernel,
        out_shape=(shape((64, 8, 128), BF), shape((48, 512), BF)),
        in_specs=[SMEM] * 2 + [VMEM] * 7,
        out_specs=(VMEM, VMEM),
        scratch_shapes=[
            pltpu.VMEM((3, 1024, 512), BF),
            pltpu.VMEM((3, 1024, 1024), BF),
            pltpu.VMEM((3, 1024, 128), F32),
            pltpu.VMEM((288, 1024), BF),
            pltpu.VMEM((288, 1024), BF),
            pltpu.VMEM((512, 1024), BF),
            pltpu.VMEM((4, 288, 512), F32),
            pltpu.VMEM((4, 288, 512), F32),
            pltpu.VMEM((4, 288, 512), BF),
            pltpu.VMEM((48, 1024), F32),
            pltpu.VMEM((3, 8, 1536), F32),
        ],
        compiler_params=pltpu.CompilerParams(vmem_limit_bytes=44 << 20),
        name="sweep",
    )(
        col,
        tile_class,
        pack,
        points,
        area.reshape(1, 1024),
        connect,
        node_coords,
        fronts,
        slots,
    )
    core = lax.ppermute(node_part, ROW, [(i, i ^ 1) for i in range(4)])
    side = lax.ppermute(node_part, ROW, [(i, i ^ 2) for i in range(4)])
    cross = lax.ppermute(node_part, ROW, [(i, i ^ 3) for i in range(4)])
    front_sum = lax.all_to_all(front_part, COL, 0, 0)
    front_grad, node_grad = pl.pallas_call(
        last_kernel,
        out_shape=(shape((16, 48), F32), shape((48, 512), F32)),
        in_specs=[VMEM] * 5,
        out_specs=(VMEM, VMEM),
        compiler_params=pltpu.CompilerParams(vmem_limit_bytes=16 << 20),
        name="last",
    )(front_sum, node_part, core, side, cross)
    return (front_grad, node_grad.T)


def solution(mesh):
    fine = Mesh(mesh.devices.reshape(2, 2, 8, 2, 4), ROW + COL)
    in_specs = (
        P(COL, ROW),
        P(COL, ROW),
        P(COL),
        P(None, COL),
        P(None, COL),
        P(ROW),
        P(ROW, COL),
    )
    out_specs = (P(ROW + COL, None), P(COL, None))
    return jax.shard_map(body, mesh=fine, in_specs=in_specs, out_specs=out_specs, check_vma=False)
```

```python
import jax
import jax.numpy as jnp
from jax import lax
from jax.experimental import pallas as pl
from jax.experimental.pallas import tpu as pltpu
from jax.sharding import Mesh, PartitionSpec as P

SOFTEN = 0.05
COL = ("z", "yh", "x")
ROW = ("yl", "co")
BF = jnp.bfloat16
F32 = jnp.float32

NT = (((1,), (1,)), ((), ()))
TN = (((0,), (0,)), ((), ()))


def iota(shape, dim):
    return lax.broadcasted_iota(jnp.int32, shape, dim)


def one_hot(mask):
    return jnp.where(mask, 1.0, 0.0).astype(BF)


CAP = 40
CAP_PART = 16
FAST = 1
SLOTS = 176
SLOT_PART = 64


def ranks(owner):
    column = one_hot(iota((64, 1024), 0) == owner)
    group = one_hot(iota((16, 1024), 0) == (owner & 7))
    both = jnp.concatenate([column, group], 0)
    ahead = one_hot(iota((1024, 1024), 0) < iota((1024, 1024), 1))
    before = jnp.dot(both, ahead, preferred_element_type=F32) * both.astype(F32)
    inner = jnp.sum(before[:64], axis=0, keepdims=True).astype(jnp.int32)
    outer = jnp.sum(before[64:], axis=0, keepdims=True).astype(jnp.int32)
    return inner, outer


def take(slot, count, value):
    hit = jnp.where(iota((count, 1024), 0) == slot, value + 1.0, 0.0)
    return jnp.sum(hit, axis=1, keepdims=True) - 1.0


def prep_kernel(col_ref, gathered_ref, connect_ref, coords_ref, list_ref, pack_ref, points_ref, table_ref, pool_ref, place_ref, fits_ref):
    col = col_ref[0]
    place = iota((288, 320), 0)
    source = iota((288, 320), 1)
    group = place >> 4
    load = place & 15
    half = jnp.where(group >= 9, 1, 0)
    comp = group - 9 * half
    wanted = (load >> 2) * 80 + half * 36 + (load & 3) * 9 + comp
    permute = one_hot(source == wanted)
    gathered = gathered_ref[...].reshape(320, 1024)
    pack = jnp.dot(permute, gathered, preferred_element_type=F32).astype(BF)
    pack_ref[...] = pack
    base = jnp.concatenate([coords_ref[...].astype(F32), jnp.zeros((13, 512), F32)], 0)
    points = jnp.zeros((16, 1024), F32)
    for corner in range(3):
        chosen = one_hot(iota((512, 1024), 0) == connect_ref[corner : corner + 1, :] - col * 512)
        shifted = base if corner == 0 else pltpu.roll(base, 3 * corner, 0)
        points = points + jnp.dot(shifted.astype(BF), chosen, preferred_element_type=F32)
    points_ref[...] = points
    table = jnp.concatenate([pack[144:], pack[:144], points.astype(BF)], 0)
    table_ref[...] = table

    most = jnp.zeros((64, 1), F32)
    crowd = jnp.zeros((8, 1), F32)
    for r in range(4):
        owner = gathered[80 * r + 72 : 80 * r + 73, :].astype(jnp.int32) >> 2
        count = jnp.sum(jnp.where(iota((64, 1024), 0) == owner, 1.0, 0.0), axis=1, keepdims=True)
        most = jnp.maximum(most, count)
        crowd = jnp.maximum(crowd, jnp.sum(count.reshape(8, 8, 1), axis=0))
    fits = jnp.logical_and(jnp.max(most) <= CAP, jnp.max(crowd) <= SLOTS)
    fits_ref[0, 0] = jnp.where(fits, 1, 0).astype(jnp.int32)

    owner = list_ref[...] >> 10
    inner, outer = ranks(owner)
    place_ref[0:1, :] = (owner >> 3) * CAP + inner
    place_ref[1:2, :] = (owner & 7) * SLOTS + outer
    local = (list_ref[...] & 1023).astype(F32)
    slot = jnp.where(owner == col, inner, -1)
    chosen = take(slot, CAP, local).astype(jnp.int32)
    chosen = one_hot(iota((CAP, 1024), 1) == chosen)
    picked = lax.dot_general(chosen, table, NT, preferred_element_type=F32)
    picked = jnp.concatenate([picked, jnp.zeros((CAP, 80), F32)], 1)
    pool_ref[...] = jnp.broadcast_to(fold(picked, CAP, CAP_PART).astype(BF)[None], pool_ref.shape)


def fold(rows, count, part):
    third = jnp.concatenate([rows[:, 256:384], jnp.zeros((3 * part - count, 128), F32)], 0)
    third = (
        third[:part]
        + pltpu.roll(third[part : 2 * part], 42, 1)
        + pltpu.roll(third[2 * part :], 84, 1)
    )
    return jnp.concatenate([rows[:, 0:128], rows[:, 128:256], third], 0)


def unfold(pool, groups, count, part):
    first = pool[:, 2 * count :, :]
    flat = first.reshape(groups * part, 128)
    second = pltpu.roll(flat, 86, 1).reshape(groups, part, 128)
    third = pltpu.roll(flat, 44, 1).reshape(groups, part, 128)
    third = jnp.concatenate([first, second, third[:, : count - 2 * part]], 1)
    blocks = [pool[:, 0:count, :], pool[:, count : 2 * count, :], third]
    return jnp.concatenate([block.reshape(groups * count, 128) for block in blocks], 1)


def merge_kernel(col_ref, pool_ref, place_ref, out_ref):
    mine = (col_ref[0] & 7) * SLOTS
    outer = place_ref[1:2, :] - mine
    chosen = take(outer, SLOTS, place_ref[0:1, :].astype(F32)).astype(jnp.int32)
    chosen = one_hot(iota((SLOTS, 8 * CAP), 1) == chosen)
    rows = unfold(pool_ref[...].astype(F32), 8, CAP, CAP_PART).astype(BF)
    rows = jnp.dot(chosen, rows, preferred_element_type=F32)
    rows = jnp.where(iota((SLOTS, 384), 1) < 298, rows, 0.0)
    out_ref[...] = jnp.broadcast_to(fold(rows, SLOTS, SLOT_PART).astype(BF)[None], out_ref.shape)


def whole_kernel(col_ref, table_ref, list_ref, rows_ref):
    owned = one_hot(iota((1024, 1024), 0) == list_ref[...] - col_ref[0] * 1024)
    picked = jnp.dot(table_ref[...], owned, preferred_element_type=F32)
    picked = jnp.concatenate([picked, jnp.zeros((80, 1024), F32)], 0)
    rows_ref[...] = jnp.transpose(picked).astype(BF)


def load_sum(product, count):
    return jnp.sum(product.reshape(18, 16, count), axis=0)


def main_kernel(
    col_ref,
    class_ref,
    pack_ref,
    points_ref,
    area_ref,
    connect_ref,
    coords_ref,
    pool_ref,
    slot_ref,
    front_ref,
    node_ref,
    knode_ref,
    kcell_ref,
    frontx_ref,
    fpack_ref,
    share_ref,
    touch_ref,
    part_ref,
    nsum_ref,
    nhalf_ref,
    elem_ref,
    place_ref,
):
    scale = (4096 * 65536) ** (-0.25) / 3.0
    weight = area_ref[...] * scale
    share_ref[...] = (pack_ref[...].astype(F32) * weight).astype(BF)
    ends = [jnp.broadcast_to(connect_ref[a : a + 1, :] - col_ref[0] * 512, (16, 1024)) for a in range(3)]

    def mark(step):
        node = iota((16, 1024), 0) + 16 * step
        hit = (node == ends[0]) | (node == ends[1]) | (node == ends[2])
        touch_ref[16 * step : 16 * step + 16, :] = one_hot(hit)

    for step in range(32):
        mark(step)

    pool = jnp.transpose(unfold(pool_ref[...], 8, SLOTS, SLOT_PART))[:304]
    chosen = one_hot(iota((8 * SLOTS, 1024), 0) == slot_ref[1:2, :])
    found = jnp.dot(pool, chosen, preferred_element_type=F32)
    fpack_ref[...] = found[:288].astype(BF)
    tail = found[288:304]
    tail = [(tail[k : k + 1] + tail[3 + k : 4 + k] + tail[6 + k : 7 + k]) / 3.0 for k in range(3)]
    tail = jnp.transpose(jnp.concatenate(tail + [jnp.zeros((5, 1024), F32)], 0))
    for k in range(3):
        frontx_ref[k] = jnp.broadcast_to(tail[:, k : k + 1], (1024, 128))
    rows = [[points_ref[3 * a + k : 3 * a + k + 1, :] for k in range(3)] for a in range(3)]
    center = [(rows[0][k] + rows[1][k] + rows[2][k]) / 3.0 for k in range(3)]
    corner = [coords_ref[k : k + 1, :].astype(F32) for k in range(3)]

    mask = [[class_ref[it, jt].astype(F32) for jt in range(4)] for it in range(4)]

    for k in range(3):
        place_ref[k, :, 0:512] = jnp.broadcast_to(corner[k], (8, 512))
        place_ref[k, :, 512:1536] = jnp.broadcast_to(center[k], (8, 1024))

    def fill(out_ref, step, lanes, shift, soften):
        at = slice(16 * step, 16 * step + 16)
        offset = []
        for k in range(3):
            piece = frontx_ref[k, at, :]
            place = place_ref[k, :, lanes.start + shift : lanes.stop + shift]
            place = jnp.concatenate([place, place], 0)
            offset.append(jnp.concatenate([piece, piece], 1) - place)
        squared = offset[0] * offset[0] + offset[1] * offset[1] + offset[2] * offset[2] + soften
        inverse = lax.rsqrt(squared)
        factor = inverse * inverse * inverse
        for k in range(3):
            out_ref[k, at, lanes] = (offset[k] * factor).astype(BF)

    def weave(many, few):
        done = 0
        for place, job in enumerate(many):
            while done < len(few) and done * len(many) <= place * len(few):
                few[done]()
                done += 1
            job()
        for job in few[done:]:
            job()

    def part(jt):
        lanes = slice(256 * jt, 256 * jt + 256)
        part_ref[jt] = lax.dot_general(
            share_ref[:, lanes], touch_ref[:, lanes], NT, preferred_element_type=F32
        )

    def node_fill(step, half):
        fill(knode_ref, step, slice(256 * half, 256 * half + 256), 0, SOFTEN)

    def cell_fill(step, jt):
        soften = jnp.where(class_ref[step // 16, jt] == 1, 3.0e38, SOFTEN).astype(F32)
        fill(kcell_ref, step, slice(256 * jt, 256 * jt + 256), 512, soften)

    weave(
        [lambda s=s, h=h: node_fill(s, h) for h in range(2) for s in range(64)],
        [lambda jt=jt: part(jt) for jt in range(4)],
    )

    def blend(step):
        at = slice(16 * step, 16 * step + 16)
        part = [part_ref[jt, at, :] for jt in range(4)]
        for it in range(4):
            total = part[0] * mask[it][0]
            for jt in range(1, 4):
                total = total + part[jt] * mask[it][jt]
            nsum_ref[it, at, :] = total
            nhalf_ref[it, at, :] = total.astype(BF)

    nodes = [[], [], []]

    def node_dot(k, it):
        rows = slice(256 * it, 256 * it + 256)
        product = jnp.dot(fpack_ref[:, rows], knode_ref[k, rows, :], preferred_element_type=F32)
        nodes[k].append(load_sum(product * nsum_ref[it], 512))

    def cell_dot(k, jt):
        lanes = slice(256 * jt, 256 * jt + 256)
        leader = pack_ref[:, lanes].astype(F32) * weight[:, lanes]
        product = jnp.dot(fpack_ref[...], kcell_ref[k, :, lanes], preferred_element_type=F32)
        elem_ref[16 * k : 16 * k + 16, lanes] = load_sum(product * leader, 256)

    weave(
        [lambda s=s, jt=jt: cell_fill(s, jt) for jt in range(2) for s in range(64)],
        [lambda s=s: blend(s) for s in range(18)]
        + [lambda k=k, it=it: node_dot(k, it) for k in range(3) for it in range(4)]
        + [lambda k=k: cell_dot(k, 0) for k in range(3)],
    )

    pieces = [[] for it in range(4)]

    def row_dot(k, it):
        rows = slice(256 * it, 256 * it + 256)
        product = 3.0 * lax.dot_general(
            share_ref[...], kcell_ref[k, rows, :], NT, preferred_element_type=F32
        ) + lax.dot_general(nhalf_ref[it], knode_ref[k, rows, :], NT, preferred_element_type=F32)
        pieces[it].append(-load_sum(product * fpack_ref[:, rows].astype(F32), 256))

    for it in range(4):
        if it == 0:
            few = [lambda k=k: cell_dot(k, 1) for k in range(3)]
        else:
            few = [lambda k=k, it=it: row_dot(k, it - 1) for k in range(3)]
        weave([lambda s=s, jt=jt, it=it: cell_fill(16 * it + s, jt) for s in range(16) for jt in (2, 3)], few)
    for k in range(3):
        row_dot(k, 3)
    for jt in (2, 3):
        for k in range(3):
            cell_dot(k, jt)
    nodes = jnp.concatenate([part[0] + part[1] + part[2] + part[3] for part in nodes], 0)
    value = elem_ref[...]
    high = value.astype(BF)
    low = (value - high.astype(F32)).astype(BF)
    spread = lax.dot_general(
        jnp.concatenate([high, low], 0), touch_ref[...], NT, preferred_element_type=F32
    )
    node_ref[...] = (nodes + (spread[:48] + spread[48:])).astype(BF)

    columns = []
    for it in range(4):
        filled = jnp.concatenate(pieces[it] + [jnp.zeros((80, 256), F32)], 0)
        columns.append(jnp.transpose(filled))
    turned = jnp.concatenate(columns, 0).reshape(64, 16, 128)
    packed = turned[:, :8] + pltpu.roll(turned[:, 8:].reshape(512, 128), 64, 1).reshape(64, 8, 128)
    front_ref[...] = packed.astype(BF)


def last_kernel(front_ref, own_ref, core_ref, side_ref, cross_ref, out_front_ref, out_node_ref):
    total = jnp.sum(front_ref[...].astype(F32), axis=0)
    out_front_ref[0:8, :] = total[:, 0:48]
    out_front_ref[8:16, :] = pltpu.roll(total, 64, 1)[:, 0:48]
    near = own_ref[...].astype(F32) + core_ref[...].astype(F32)
    far = side_ref[...].astype(F32) + cross_ref[...].astype(F32)
    out_node_ref[...] = near + far


def shape(dims, dtype):
    return jax.ShapeDtypeStruct(dims, dtype)


VMEM = pl.BlockSpec(memory_space=pltpu.VMEM)
SMEM = pl.BlockSpec(memory_space=pltpu.SMEM)


def body(state, adjoint, area, node_coords, connect, front_list, tile_class):
    col = lax.axis_index(COL).astype(jnp.int32).reshape(1)
    front_list = front_list.reshape(1, 1024)
    owners = (front_list >> 8).astype(BF)
    mine = jnp.concatenate([state.T, adjoint.T, owners, jnp.zeros((7, 1024), BF)], 0)
    gathered = lax.all_gather(mine, ROW)
    pack, points, table, pool, place, fits = pl.pallas_call(
        prep_kernel,
        out_shape=(
            shape((288, 1024), BF),
            shape((16, 1024), F32),
            shape((304, 1024), BF),
            shape((8, 2 * CAP + CAP_PART, 128), BF),
            shape((2, 1024), jnp.int32),
            shape((1, 1), jnp.int32),
        ),
        in_specs=[SMEM] + [VMEM] * 4,
        out_specs=(VMEM, VMEM, VMEM, VMEM, VMEM, SMEM),
        compiler_params=pltpu.CompilerParams(vmem_limit_bytes=24 << 20),
        name="prep",
    )(col, gathered, connect, node_coords, front_list)

    def compact(pool, place, table):
        part = lax.all_to_all(pool, "z", 0, 0)
        merged = pl.pallas_call(
            merge_kernel,
            out_shape=shape((8, 2 * SLOTS + SLOT_PART, 128), BF),
            in_specs=[SMEM] + [VMEM] * 2,
            out_specs=VMEM,
            compiler_params=pltpu.CompilerParams(vmem_limit_bytes=24 << 20),
            name="merge",
        )(col, part, place)
        return lax.all_to_all(merged, ("yh", "x"), 0, 0), place

    def whole(pool, place, table):
        rows = pl.pallas_call(
            whole_kernel,
            out_shape=shape((1024, 384), BF),
            in_specs=[SMEM] + [VMEM] * 2,
            out_specs=VMEM,
            name="whole",
        )(col, table, front_list)
        part = lax.all_to_all(rows.reshape(64, 16, 384), COL, 0, 0)
        share = jnp.sum(part, axis=0, dtype=BF)
        spread = jnp.broadcast_to(share[None], (64, 16, 384))
        rows = lax.all_to_all(spread, COL, 0, 0).reshape(1024, 384)
        rows = jnp.pad(rows, ((0, 8 * SLOTS - 1024), (0, 0))).reshape(8, SLOTS, 384)
        third = jnp.pad(rows[:, :, 256:298], ((0, 0), (0, 3 * SLOT_PART - SLOTS), (0, 0)))
        third = third.reshape(8, 3, SLOT_PART, 42)
        third = jnp.concatenate([third[:, 0], third[:, 1], third[:, 2]], 2)
        third = jnp.pad(third, ((0, 0), (0, 0), (0, 2)))
        pool = jnp.concatenate([rows[:, :, 0:128], rows[:, :, 128:256], third], 1)
        return pool, jnp.broadcast_to(jnp.arange(1024, dtype=jnp.int32), (2, 1024))

    fronts, slots = lax.cond(fits[0, 0] == FAST, compact, whole, pool, place, table)
    front_part, node_part = pl.pallas_call(
        main_kernel,
        out_shape=(shape((64, 8, 128), BF), shape((48, 512), BF)),
        in_specs=[SMEM] * 2 + [VMEM] * 7,
        out_specs=(VMEM, VMEM),
        scratch_shapes=[
            pltpu.VMEM((3, 1024, 512), BF),
            pltpu.VMEM((3, 1024, 1024), BF),
            pltpu.VMEM((3, 1024, 128), F32),
            pltpu.VMEM((288, 1024), BF),
            pltpu.VMEM((288, 1024), BF),
            pltpu.VMEM((512, 1024), BF),
            pltpu.VMEM((4, 288, 512), F32),
            pltpu.VMEM((4, 288, 512), F32),
            pltpu.VMEM((4, 288, 512), BF),
            pltpu.VMEM((48, 1024), F32),
            pltpu.VMEM((3, 8, 1536), F32),
        ],
        compiler_params=pltpu.CompilerParams(vmem_limit_bytes=44 << 20),
        name="sweep",
    )(
        col,
        tile_class,
        pack,
        points,
        area.reshape(1, 1024),
        connect,
        node_coords,
        fronts,
        slots,
    )
    core = lax.ppermute(node_part, ROW, [(i, i ^ 1) for i in range(4)])
    side = lax.ppermute(node_part, ROW, [(i, i ^ 2) for i in range(4)])
    cross = lax.ppermute(node_part, ROW, [(i, i ^ 3) for i in range(4)])
    front_sum = lax.all_to_all(front_part, COL, 0, 0)
    front_grad, node_grad = pl.pallas_call(
        last_kernel,
        out_shape=(shape((16, 48), F32), shape((48, 512), F32)),
        in_specs=[VMEM] * 5,
        out_specs=(VMEM, VMEM),
        compiler_params=pltpu.CompilerParams(vmem_limit_bytes=16 << 20),
        name="last",
    )(front_sum, node_part, core, side, cross)
    return (front_grad, node_grad.T)


def solution(mesh):
    fine = Mesh(mesh.devices.reshape(2, 2, 8, 2, 4), ROW + COL)
    in_specs = (
        P(COL, ROW),
        P(COL, ROW),
        P(COL),
        P(None, COL),
        P(None, COL),
        P(ROW),
        P(ROW, COL),
    )
    out_specs = (P(ROW + COL, None), P(COL, None))
    return jax.shard_map(body, mesh=fine, in_specs=in_specs, out_specs=out_specs, check_vma=False)
```

```python
import jax
import jax.numpy as jnp
from jax import lax
from jax.experimental import pallas as pl
from jax.experimental.pallas import tpu as pltpu
from jax.sharding import Mesh, PartitionSpec as P

SOFTEN = 0.05
COL = ("z", "yh", "x")
ROW = ("yl", "co")
BF = jnp.bfloat16
F32 = jnp.float32

NT = (((1,), (1,)), ((), ()))
TN = (((0,), (0,)), ((), ()))


def iota(shape, dim):
    return lax.broadcasted_iota(jnp.int32, shape, dim)


def one_hot(mask):
    return jnp.where(mask, 1.0, 0.0).astype(BF)


CAP = 40
CAP_PART = 16
FAST = 1
SLOTS = 176
SLOT_PART = 64


def ranks(owner):
    column = one_hot(iota((64, 1024), 0) == owner)
    group = one_hot(iota((16, 1024), 0) == (owner & 7))
    both = jnp.concatenate([column, group], 0)
    ahead = one_hot(iota((1024, 1024), 0) < iota((1024, 1024), 1))
    before = jnp.dot(both, ahead, preferred_element_type=F32) * both.astype(F32)
    inner = jnp.sum(before[:64], axis=0, keepdims=True).astype(jnp.int32)
    outer = jnp.sum(before[64:], axis=0, keepdims=True).astype(jnp.int32)
    return inner, outer


def take(slot, count, value):
    hit = jnp.where(iota((count, 1024), 0) == slot, value + 1.0, 0.0)
    return jnp.sum(hit, axis=1, keepdims=True) - 1.0


def prep_kernel(col_ref, gathered_ref, connect_ref, coords_ref, list_ref, pack_ref, points_ref, table_ref, pool_ref, place_ref, fits_ref):
    col = col_ref[0]
    place = iota((288, 320), 0)
    source = iota((288, 320), 1)
    group = place >> 4
    load = place & 15
    half = jnp.where(group >= 9, 1, 0)
    comp = group - 9 * half
    wanted = (load >> 2) * 80 + half * 36 + (load & 3) * 9 + comp
    permute = one_hot(source == wanted)
    gathered = gathered_ref[...].reshape(320, 1024)
    pack = jnp.dot(permute, gathered, preferred_element_type=F32).astype(BF)
    pack_ref[...] = pack
    base = jnp.concatenate([coords_ref[...].astype(F32), jnp.zeros((13, 512), F32)], 0)
    points = jnp.zeros((16, 1024), F32)
    for corner in range(3):
        chosen = one_hot(iota((512, 1024), 0) == connect_ref[corner : corner + 1, :] - col * 512)
        shifted = base if corner == 0 else pltpu.roll(base, 3 * corner, 0)
        points = points + jnp.dot(shifted.astype(BF), chosen, preferred_element_type=F32)
    points_ref[...] = points
    table = jnp.concatenate([pack[144:], pack[:144], points.astype(BF)], 0)
    table_ref[...] = table

    most = jnp.zeros((64, 1), F32)
    crowd = jnp.zeros((8, 1), F32)
    for r in range(4):
        owner = gathered[80 * r + 72 : 80 * r + 73, :].astype(jnp.int32) >> 2
        count = jnp.sum(jnp.where(iota((64, 1024), 0) == owner, 1.0, 0.0), axis=1, keepdims=True)
        most = jnp.maximum(most, count)
        crowd = jnp.maximum(crowd, jnp.sum(count.reshape(8, 8, 1), axis=0))
    fits = jnp.logical_and(jnp.max(most) <= CAP, jnp.max(crowd) <= SLOTS)
    fits_ref[0, 0] = jnp.where(fits, 1, 0).astype(jnp.int32)

    owner = list_ref[...] >> 10
    inner, outer = ranks(owner)
    place_ref[0:1, :] = (owner >> 3) * CAP + inner
    place_ref[1:2, :] = (owner & 7) * SLOTS + outer
    local = (list_ref[...] & 1023).astype(F32)
    slot = jnp.where(owner == col, inner, -1)
    chosen = take(slot, CAP, local).astype(jnp.int32)
    chosen = one_hot(iota((CAP, 1024), 1) == chosen)
    picked = lax.dot_general(chosen, table, NT, preferred_element_type=F32)
    picked = jnp.concatenate([picked, jnp.zeros((CAP, 80), F32)], 1)
    pool_ref[...] = jnp.broadcast_to(fold(picked, CAP, CAP_PART).astype(BF)[None], pool_ref.shape)


def fold(rows, count, part):
    third = jnp.concatenate([rows[:, 256:384], jnp.zeros((3 * part - count, 128), F32)], 0)
    third = (
        third[:part]
        + pltpu.roll(third[part : 2 * part], 42, 1)
        + pltpu.roll(third[2 * part :], 84, 1)
    )
    return jnp.concatenate([rows[:, 0:128], rows[:, 128:256], third], 0)


def unfold(pool, groups, count, part):
    first = pool[:, 2 * count :, :]
    flat = first.reshape(groups * part, 128)
    second = pltpu.roll(flat, 86, 1).reshape(groups, part, 128)
    third = pltpu.roll(flat, 44, 1).reshape(groups, part, 128)
    third = jnp.concatenate([first, second, third[:, : count - 2 * part]], 1)
    blocks = [pool[:, 0:count, :], pool[:, count : 2 * count, :], third]
    return jnp.concatenate([block.reshape(groups * count, 128) for block in blocks], 1)


def merge_kernel(col_ref, pool_ref, place_ref, out_ref):
    mine = (col_ref[0] & 7) * SLOTS
    outer = place_ref[1:2, :] - mine
    chosen = take(outer, SLOTS, place_ref[0:1, :].astype(F32)).astype(jnp.int32)
    chosen = one_hot(iota((SLOTS, 8 * CAP), 1) == chosen)
    rows = unfold(pool_ref[...].astype(F32), 8, CAP, CAP_PART).astype(BF)
    rows = jnp.dot(chosen, rows, preferred_element_type=F32)
    rows = jnp.where(iota((SLOTS, 384), 1) < 298, rows, 0.0)
    out_ref[...] = jnp.broadcast_to(fold(rows, SLOTS, SLOT_PART).astype(BF)[None], out_ref.shape)


def whole_kernel(col_ref, table_ref, list_ref, rows_ref):
    owned = one_hot(iota((1024, 1024), 0) == list_ref[...] - col_ref[0] * 1024)
    picked = jnp.dot(table_ref[...], owned, preferred_element_type=F32)
    picked = jnp.concatenate([picked, jnp.zeros((80, 1024), F32)], 0)
    rows_ref[...] = jnp.transpose(picked).astype(BF)


def load_sum(product, count):
    return jnp.sum(product.reshape(18, 16, count), axis=0)


def main_kernel(
    col_ref,
    class_ref,
    pack_ref,
    points_ref,
    area_ref,
    connect_ref,
    coords_ref,
    pool_ref,
    slot_ref,
    front_ref,
    node_ref,
    knode_ref,
    kcell_ref,
    frontx_ref,
    fpack_ref,
    share_ref,
    touch_ref,
    part_ref,
    nsum_ref,
    nhalf_ref,
    elem_ref,
    place_ref,
):
    scale = (4096 * 65536) ** (-0.25) / 3.0
    weight = area_ref[...] * scale
    share_ref[...] = (pack_ref[...].astype(F32) * weight).astype(BF)
    ends = [jnp.broadcast_to(connect_ref[a : a + 1, :] - col_ref[0] * 512, (16, 1024)) for a in range(3)]

    def mark(step):
        node = iota((16, 1024), 0) + 16 * step
        hit = (node == ends[0]) | (node == ends[1]) | (node == ends[2])
        touch_ref[16 * step : 16 * step + 16, :] = one_hot(hit)

    for step in range(32):
        mark(step)

    pool = jnp.transpose(unfold(pool_ref[...], 8, SLOTS, SLOT_PART))[:304]
    chosen = one_hot(iota((8 * SLOTS, 1024), 0) == slot_ref[1:2, :])
    found = jnp.dot(pool, chosen, preferred_element_type=F32)
    fpack_ref[...] = found[:288].astype(BF)
    tail = found[288:304]
    tail = [(tail[k : k + 1] + tail[3 + k : 4 + k] + tail[6 + k : 7 + k]) / 3.0 for k in range(3)]
    tail = jnp.transpose(jnp.concatenate(tail + [jnp.zeros((5, 1024), F32)], 0))
    for k in range(3):
        frontx_ref[k] = jnp.broadcast_to(tail[:, k : k + 1], (1024, 128))
    rows = [[points_ref[3 * a + k : 3 * a + k + 1, :] for k in range(3)] for a in range(3)]
    center = [(rows[0][k] + rows[1][k] + rows[2][k]) / 3.0 for k in range(3)]
    corner = [coords_ref[k : k + 1, :].astype(F32) for k in range(3)]

    mask = [[class_ref[it, jt].astype(F32) for jt in range(4)] for it in range(4)]

    for k in range(3):
        place_ref[k, :, 0:512] = jnp.broadcast_to(corner[k], (8, 512))
        place_ref[k, :, 512:1536] = jnp.broadcast_to(center[k], (8, 1024))

    def fill(out_ref, step, lanes, shift, soften):
        at = slice(16 * step, 16 * step + 16)
        offset = []
        for k in range(3):
            piece = frontx_ref[k, at, :]
            place = place_ref[k, :, lanes.start + shift : lanes.stop + shift]
            place = jnp.concatenate([place, place], 0)
            offset.append(jnp.concatenate([piece, piece], 1) - place)
        squared = offset[0] * offset[0] + offset[1] * offset[1] + offset[2] * offset[2] + soften
        inverse = lax.rsqrt(squared)
        factor = inverse * inverse * inverse
        for k in range(3):
            out_ref[k, at, lanes] = (offset[k] * factor).astype(BF)

    def weave(many, few):
        done = 0
        for place, job in enumerate(many):
            while done < len(few) and done * len(many) <= place * len(few):
                few[done]()
                done += 1
            job()
        for job in few[done:]:
            job()

    def part(jt):
        lanes = slice(256 * jt, 256 * jt + 256)
        part_ref[jt] = lax.dot_general(
            share_ref[:, lanes], touch_ref[:, lanes], NT, preferred_element_type=F32
        )

    def node_fill(step, half):
        fill(knode_ref, step, slice(256 * half, 256 * half + 256), 0, SOFTEN)

    def cell_fill(step, jt):
        soften = jnp.where(class_ref[step // 16, jt] == 1, 3.0e38, SOFTEN).astype(F32)
        fill(kcell_ref, step, slice(256 * jt, 256 * jt + 256), 512, soften)

    def blend(step):
        at = slice(16 * step, 16 * step + 16)
        part = [part_ref[jt, at, :] for jt in range(4)]
        for it in range(4):
            total = part[0] * mask[it][0]
            for jt in range(1, 4):
                total = total + part[jt] * mask[it][jt]
            nsum_ref[it, at, :] = total
            nhalf_ref[it, at, :] = total.astype(BF)

    nodes = [[], [], []]

    def node_dot(k, it):
        rows = slice(256 * it, 256 * it + 256)
        product = jnp.dot(fpack_ref[:, rows], knode_ref[k, rows, :], preferred_element_type=F32)
        nodes[k].append(load_sum(product * nsum_ref[it], 512))

    def cell_dot(k, jt):
        lanes = slice(256 * jt, 256 * jt + 256)
        leader = pack_ref[:, lanes].astype(F32) * weight[:, lanes]
        product = jnp.dot(fpack_ref[...], kcell_ref[k, :, lanes], preferred_element_type=F32)
        elem_ref[16 * k : 16 * k + 16, lanes] = load_sum(product * leader, 256)

    cells = [[] for it in range(4)]
    pieces = [[] for it in range(4)]

    def row_cell(k, it):
        rows = slice(256 * it, 256 * it + 256)
        product = lax.dot_general(share_ref[...], kcell_ref[k, rows, :], NT, preferred_element_type=F32)
        cells[it].append(load_sum(product * fpack_ref[:, rows].astype(F32), 256))

    def row_node(k, it):
        rows = slice(256 * it, 256 * it + 256)
        product = lax.dot_general(nhalf_ref[it], knode_ref[k, rows, :], NT, preferred_element_type=F32)
        value = load_sum(product * fpack_ref[:, rows].astype(F32), 256)
        pieces[it].append(-(value + 3.0 * cells[it][k]))

    for it in range(4):
        if it == 0:
            few = [lambda jt=jt: part(jt) for jt in range(4)]
        else:
            few = [lambda k=k, it=it: row_cell(k, it - 1) for k in range(3)]
        weave([lambda s=s, jt=jt, it=it: cell_fill(16 * it + s, jt) for s in range(16) for jt in range(4)], few)
    many = []
    for s in range(64):
        many += [lambda s=s, h=h: node_fill(s, h) for h in range(2)]
        if s % 3 == 0 and s // 3 < 18:
            many.append(lambda s=s: blend(s // 3))
    weave(
        many,
        [lambda k=k: row_cell(k, 3) for k in range(3)]
        + [lambda k=k, jt=jt: cell_dot(k, jt) for jt in range(4) for k in range(3)],
    )
    for it in range(4):
        for k in range(3):
            node_dot(k, it)
            row_node(k, it)
    nodes = jnp.concatenate([part[0] + part[1] + part[2] + part[3] for part in nodes], 0)
    value = elem_ref[...]
    high = value.astype(BF)
    low = (value - high.astype(F32)).astype(BF)
    spread = lax.dot_general(
        jnp.concatenate([high, low], 0), touch_ref[...], NT, preferred_element_type=F32
    )
    node_ref[...] = (nodes + (spread[:48] + spread[48:])).astype(BF)

    columns = []
    for it in range(4):
        filled = jnp.concatenate(pieces[it] + [jnp.zeros((80, 256), F32)], 0)
        columns.append(jnp.transpose(filled))
    turned = jnp.concatenate(columns, 0).reshape(64, 16, 128)
    packed = turned[:, :8] + pltpu.roll(turned[:, 8:].reshape(512, 128), 64, 1).reshape(64, 8, 128)
    front_ref[...] = packed.astype(BF)


def last_kernel(front_ref, own_ref, core_ref, side_ref, cross_ref, out_front_ref, out_node_ref):
    total = jnp.sum(front_ref[...].astype(F32), axis=0)
    out_front_ref[0:8, :] = total[:, 0:48]
    out_front_ref[8:16, :] = pltpu.roll(total, 64, 1)[:, 0:48]
    near = own_ref[...].astype(F32) + core_ref[...].astype(F32)
    far = side_ref[...].astype(F32) + cross_ref[...].astype(F32)
    out_node_ref[...] = near + far


def shape(dims, dtype):
    return jax.ShapeDtypeStruct(dims, dtype)


VMEM = pl.BlockSpec(memory_space=pltpu.VMEM)
SMEM = pl.BlockSpec(memory_space=pltpu.SMEM)


def body(state, adjoint, area, node_coords, connect, front_list, tile_class):
    col = lax.axis_index(COL).astype(jnp.int32).reshape(1)
    front_list = front_list.reshape(1, 1024)
    owners = (front_list >> 8).astype(BF)
    mine = jnp.concatenate([state.T, adjoint.T, owners, jnp.zeros((7, 1024), BF)], 0)
    gathered = lax.all_gather(mine, ROW)
    pack, points, table, pool, place, fits = pl.pallas_call(
        prep_kernel,
        out_shape=(
            shape((288, 1024), BF),
            shape((16, 1024), F32),
            shape((304, 1024), BF),
            shape((8, 2 * CAP + CAP_PART, 128), BF),
            shape((2, 1024), jnp.int32),
            shape((1, 1), jnp.int32),
        ),
        in_specs=[SMEM] + [VMEM] * 4,
        out_specs=(VMEM, VMEM, VMEM, VMEM, VMEM, SMEM),
        compiler_params=pltpu.CompilerParams(vmem_limit_bytes=24 << 20),
        name="prep",
    )(col, gathered, connect, node_coords, front_list)

    def compact(pool, place, table):
        part = lax.all_to_all(pool, "z", 0, 0)
        merged = pl.pallas_call(
            merge_kernel,
            out_shape=shape((8, 2 * SLOTS + SLOT_PART, 128), BF),
            in_specs=[SMEM] + [VMEM] * 2,
            out_specs=VMEM,
            compiler_params=pltpu.CompilerParams(vmem_limit_bytes=24 << 20),
            name="merge",
        )(col, part, place)
        return lax.all_to_all(merged, ("yh", "x"), 0, 0), place

    def whole(pool, place, table):
        rows = pl.pallas_call(
            whole_kernel,
            out_shape=shape((1024, 384), BF),
            in_specs=[SMEM] + [VMEM] * 2,
            out_specs=VMEM,
            name="whole",
        )(col, table, front_list)
        part = lax.all_to_all(rows.reshape(64, 16, 384), COL, 0, 0)
        share = jnp.sum(part, axis=0, dtype=BF)
        spread = jnp.broadcast_to(share[None], (64, 16, 384))
        rows = lax.all_to_all(spread, COL, 0, 0).reshape(1024, 384)
        rows = jnp.pad(rows, ((0, 8 * SLOTS - 1024), (0, 0))).reshape(8, SLOTS, 384)
        third = jnp.pad(rows[:, :, 256:298], ((0, 0), (0, 3 * SLOT_PART - SLOTS), (0, 0)))
        third = third.reshape(8, 3, SLOT_PART, 42)
        third = jnp.concatenate([third[:, 0], third[:, 1], third[:, 2]], 2)
        third = jnp.pad(third, ((0, 0), (0, 0), (0, 2)))
        pool = jnp.concatenate([rows[:, :, 0:128], rows[:, :, 128:256], third], 1)
        return pool, jnp.broadcast_to(jnp.arange(1024, dtype=jnp.int32), (2, 1024))

    fronts, slots = lax.cond(fits[0, 0] == FAST, compact, whole, pool, place, table)
    front_part, node_part = pl.pallas_call(
        main_kernel,
        out_shape=(shape((64, 8, 128), BF), shape((48, 512), BF)),
        in_specs=[SMEM] * 2 + [VMEM] * 7,
        out_specs=(VMEM, VMEM),
        scratch_shapes=[
            pltpu.VMEM((3, 1024, 512), BF),
            pltpu.VMEM((3, 1024, 1024), BF),
            pltpu.VMEM((3, 1024, 128), F32),
            pltpu.VMEM((288, 1024), BF),
            pltpu.VMEM((288, 1024), BF),
            pltpu.VMEM((512, 1024), BF),
            pltpu.VMEM((4, 288, 512), F32),
            pltpu.VMEM((4, 288, 512), F32),
            pltpu.VMEM((4, 288, 512), BF),
            pltpu.VMEM((48, 1024), F32),
            pltpu.VMEM((3, 8, 1536), F32),
        ],
        compiler_params=pltpu.CompilerParams(vmem_limit_bytes=44 << 20),
        name="sweep",
    )(
        col,
        tile_class,
        pack,
        points,
        area.reshape(1, 1024),
        connect,
        node_coords,
        fronts,
        slots,
    )
    core = lax.ppermute(node_part, ROW, [(i, i ^ 1) for i in range(4)])
    side = lax.ppermute(node_part, ROW, [(i, i ^ 2) for i in range(4)])
    cross = lax.ppermute(node_part, ROW, [(i, i ^ 3) for i in range(4)])
    front_sum = lax.all_to_all(front_part, COL, 0, 0)
    front_grad, node_grad = pl.pallas_call(
        last_kernel,
        out_shape=(shape((16, 48), F32), shape((48, 512), F32)),
        in_specs=[VMEM] * 5,
        out_specs=(VMEM, VMEM),
        compiler_params=pltpu.CompilerParams(vmem_limit_bytes=16 << 20),
        name="last",
    )(front_sum, node_part, core, side, cross)
    return (front_grad, node_grad.T)


def solution(mesh):
    fine = Mesh(mesh.devices.reshape(2, 2, 8, 2, 4), ROW + COL)
    in_specs = (
        P(COL, ROW),
        P(COL, ROW),
        P(COL),
        P(None, COL),
        P(None, COL),
        P(ROW),
        P(ROW, COL),
    )
    out_specs = (P(ROW + COL, None), P(COL, None))
    return jax.shard_map(body, mesh=fine, in_specs=in_specs, out_specs=out_specs, check_vma=False)
```

```python
import jax
import jax.numpy as jnp
from jax import lax
from jax.experimental import pallas as pl
from jax.experimental.pallas import tpu as pltpu
from jax.sharding import Mesh, PartitionSpec as P

SOFTEN = 0.05
COL = ("z", "yh", "x")
ROW = ("yl", "co")
BF = jnp.bfloat16
F32 = jnp.float32

NT = (((1,), (1,)), ((), ()))
TN = (((0,), (0,)), ((), ()))


def iota(shape, dim):
    return lax.broadcasted_iota(jnp.int32, shape, dim)


def one_hot(mask):
    return jnp.where(mask, 1.0, 0.0).astype(BF)


CAP = 40
CAP_PART = 16
FAST = 1
SLOTS = 176
SLOT_PART = 64


def ranks(owner):
    column = one_hot(iota((64, 1024), 0) == owner)
    group = one_hot(iota((16, 1024), 0) == (owner & 7))
    both = jnp.concatenate([column, group], 0)
    ahead = one_hot(iota((1024, 1024), 0) < iota((1024, 1024), 1))
    before = jnp.dot(both, ahead, preferred_element_type=F32) * both.astype(F32)
    inner = jnp.sum(before[:64], axis=0, keepdims=True).astype(jnp.int32)
    outer = jnp.sum(before[64:], axis=0, keepdims=True).astype(jnp.int32)
    return inner, outer


def take(slot, count, value):
    hit = jnp.where(iota((count, 1024), 0) == slot, value + 1.0, 0.0)
    return jnp.sum(hit, axis=1, keepdims=True) - 1.0


def prep_kernel(col_ref, gathered_ref, connect_ref, coords_ref, list_ref, pack_ref, points_ref, table_ref, pool_ref, place_ref, fits_ref):
    col = col_ref[0]
    place = iota((288, 320), 0)
    source = iota((288, 320), 1)
    group = place >> 4
    load = place & 15
    half = jnp.where(group >= 9, 1, 0)
    comp = group - 9 * half
    wanted = (load >> 2) * 80 + half * 36 + (load & 3) * 9 + comp
    permute = one_hot(source == wanted)
    gathered = gathered_ref[...].reshape(320, 1024)
    pack = jnp.dot(permute, gathered, preferred_element_type=F32).astype(BF)
    pack_ref[...] = pack
    base = jnp.concatenate([coords_ref[...].astype(F32), jnp.zeros((13, 512), F32)], 0)
    points = jnp.zeros((16, 1024), F32)
    for corner in range(3):
        chosen = one_hot(iota((512, 1024), 0) == connect_ref[corner : corner + 1, :] - col * 512)
        shifted = base if corner == 0 else pltpu.roll(base, 3 * corner, 0)
        points = points + jnp.dot(shifted.astype(BF), chosen, preferred_element_type=F32)
    points_ref[...] = points
    table = jnp.concatenate([pack[144:], pack[:144], points.astype(BF)], 0)
    table_ref[...] = table

    most = jnp.zeros((64, 1), F32)
    crowd = jnp.zeros((8, 1), F32)
    for r in range(4):
        owner = gathered[80 * r + 72 : 80 * r + 73, :].astype(jnp.int32) >> 2
        count = jnp.sum(jnp.where(iota((64, 1024), 0) == owner, 1.0, 0.0), axis=1, keepdims=True)
        most = jnp.maximum(most, count)
        crowd = jnp.maximum(crowd, jnp.sum(count.reshape(8, 8, 1), axis=0))
    fits = jnp.logical_and(jnp.max(most) <= CAP, jnp.max(crowd) <= SLOTS)
    fits_ref[0, 0] = jnp.where(fits, 1, 0).astype(jnp.int32)

    owner = list_ref[...] >> 10
    inner, outer = ranks(owner)
    place_ref[0:1, :] = (owner >> 3) * CAP + inner
    place_ref[1:2, :] = (owner & 7) * SLOTS + outer
    local = (list_ref[...] & 1023).astype(F32)
    slot = jnp.where(owner == col, inner, -1)
    chosen = take(slot, CAP, local).astype(jnp.int32)
    chosen = one_hot(iota((CAP, 1024), 1) == chosen)
    picked = lax.dot_general(chosen, table, NT, preferred_element_type=F32)
    picked = jnp.concatenate([picked, jnp.zeros((CAP, 80), F32)], 1)
    pool_ref[...] = jnp.broadcast_to(fold(picked, CAP, CAP_PART).astype(BF)[None], pool_ref.shape)


def fold(rows, count, part):
    third = jnp.concatenate([rows[:, 256:384], jnp.zeros((3 * part - count, 128), F32)], 0)
    third = (
        third[:part]
        + pltpu.roll(third[part : 2 * part], 42, 1)
        + pltpu.roll(third[2 * part :], 84, 1)
    )
    return jnp.concatenate([rows[:, 0:128], rows[:, 128:256], third], 0)


def unfold(pool, groups, count, part):
    first = pool[:, 2 * count :, :]
    flat = first.reshape(groups * part, 128)
    second = pltpu.roll(flat, 86, 1).reshape(groups, part, 128)
    third = pltpu.roll(flat, 44, 1).reshape(groups, part, 128)
    third = jnp.concatenate([first, second, third[:, : count - 2 * part]], 1)
    blocks = [pool[:, 0:count, :], pool[:, count : 2 * count, :], third]
    return jnp.concatenate([block.reshape(groups * count, 128) for block in blocks], 1)


def merge_kernel(col_ref, pool_ref, place_ref, out_ref):
    mine = (col_ref[0] & 7) * SLOTS
    outer = place_ref[1:2, :] - mine
    chosen = take(outer, SLOTS, place_ref[0:1, :].astype(F32)).astype(jnp.int32)
    chosen = one_hot(iota((SLOTS, 8 * CAP), 1) == chosen)
    rows = unfold(pool_ref[...].astype(F32), 8, CAP, CAP_PART).astype(BF)
    rows = jnp.dot(chosen, rows, preferred_element_type=F32)
    rows = jnp.where(iota((SLOTS, 384), 1) < 298, rows, 0.0)
    out_ref[...] = jnp.broadcast_to(fold(rows, SLOTS, SLOT_PART).astype(BF)[None], out_ref.shape)


def whole_kernel(col_ref, table_ref, list_ref, rows_ref):
    owned = one_hot(iota((1024, 1024), 0) == list_ref[...] - col_ref[0] * 1024)
    picked = jnp.dot(table_ref[...], owned, preferred_element_type=F32)
    picked = jnp.concatenate([picked, jnp.zeros((80, 1024), F32)], 0)
    rows_ref[...] = jnp.transpose(picked).astype(BF)


def load_sum(product, count):
    return jnp.sum(product.reshape(18, 16, count), axis=0)


def main_kernel(
    col_ref,
    class_ref,
    pack_ref,
    points_ref,
    area_ref,
    connect_ref,
    coords_ref,
    pool_ref,
    slot_ref,
    front_ref,
    node_ref,
    knode_ref,
    kcell_ref,
    frontx_ref,
    fpack_ref,
    share_ref,
    touch_ref,
    part_ref,
    nsum_ref,
    nhalf_ref,
    elem_ref,
    place_ref,
):
    scale = (4096 * 65536) ** (-0.25) / 3.0
    weight = area_ref[...] * scale
    share_ref[...] = (pack_ref[...].astype(F32) * weight).astype(BF)
    ends = [jnp.broadcast_to(connect_ref[a : a + 1, :] - col_ref[0] * 512, (16, 1024)) for a in range(3)]

    def mark(step):
        node = iota((16, 1024), 0) + 16 * step
        hit = (node == ends[0]) | (node == ends[1]) | (node == ends[2])
        touch_ref[16 * step : 16 * step + 16, :] = one_hot(hit)

    pool = jnp.transpose(unfold(pool_ref[...], 8, SLOTS, SLOT_PART))[:304]
    chosen = one_hot(iota((8 * SLOTS, 1024), 0) == slot_ref[1:2, :])
    found = jnp.dot(pool, chosen, preferred_element_type=F32)
    fpack_ref[...] = found[:288].astype(BF)
    tail = found[288:304]
    tail = [(tail[k : k + 1] + tail[3 + k : 4 + k] + tail[6 + k : 7 + k]) / 3.0 for k in range(3)]
    tail = jnp.transpose(jnp.concatenate(tail + [jnp.zeros((5, 1024), F32)], 0))
    for k in range(3):
        frontx_ref[k] = jnp.broadcast_to(tail[:, k : k + 1], (1024, 128))
    rows = [[points_ref[3 * a + k : 3 * a + k + 1, :] for k in range(3)] for a in range(3)]
    center = [(rows[0][k] + rows[1][k] + rows[2][k]) / 3.0 for k in range(3)]
    corner = [coords_ref[k : k + 1, :].astype(F32) for k in range(3)]

    mask = [[class_ref[it, jt].astype(F32) for jt in range(4)] for it in range(4)]

    for k in range(3):
        place_ref[k, :, 0:512] = jnp.broadcast_to(corner[k], (8, 512))
        place_ref[k, :, 512:1536] = jnp.broadcast_to(center[k], (8, 1024))

    def fill(out_ref, step, lanes, shift, soften):
        at = slice(16 * step, 16 * step + 16)
        offset = []
        for k in range(3):
            piece = frontx_ref[k, at, :]
            place = place_ref[k, :, lanes.start + shift : lanes.stop + shift]
            place = jnp.concatenate([place, place], 0)
            offset.append(jnp.concatenate([piece, piece], 1) - place)
        squared = offset[0] * offset[0] + offset[1] * offset[1] + offset[2] * offset[2] + soften
        inverse = lax.rsqrt(squared)
        factor = inverse * inverse * inverse
        for k in range(3):
            out_ref[k, at, lanes] = (offset[k] * factor).astype(BF)

    def weave(many, few):
        done = 0
        for place, job in enumerate(many):
            while done < len(few) and done * len(many) <= place * len(few):
                few[done]()
                done += 1
            job()
        for job in few[done:]:
            job()

    def part(jt):
        lanes = slice(256 * jt, 256 * jt + 256)
        part_ref[jt] = lax.dot_general(
            share_ref[:, lanes], touch_ref[:, lanes], NT, preferred_element_type=F32
        )

    def node_fill(step, half):
        fill(knode_ref, step, slice(256 * half, 256 * half + 256), 0, SOFTEN)

    def cell_fill(step, jt):
        soften = jnp.where(class_ref[step // 16, jt] == 1, 3.0e38, SOFTEN).astype(F32)
        fill(kcell_ref, step, slice(256 * jt, 256 * jt + 256), 512, soften)

    def blend(step):
        at = slice(16 * step, 16 * step + 16)
        part = [part_ref[jt, at, :] for jt in range(4)]
        for it in range(4):
            total = part[0] * mask[it][0]
            for jt in range(1, 4):
                total = total + part[jt] * mask[it][jt]
            nsum_ref[it, at, :] = total
            nhalf_ref[it, at, :] = total.astype(BF)

    nodes = [[], [], []]

    def node_dot(k, it):
        rows = slice(256 * it, 256 * it + 256)
        product = jnp.dot(fpack_ref[:, rows], knode_ref[k, rows, :], preferred_element_type=F32)
        nodes[k].append(load_sum(product * nsum_ref[it], 512))

    def cell_dot(k, jt):
        lanes = slice(256 * jt, 256 * jt + 256)
        leader = pack_ref[:, lanes].astype(F32) * weight[:, lanes]
        product = jnp.dot(fpack_ref[...], kcell_ref[k, :, lanes], preferred_element_type=F32)
        elem_ref[16 * k : 16 * k + 16, lanes] = load_sum(product * leader, 256)

    cells = [[] for it in range(4)]
    pieces = [[] for it in range(4)]

    def row_cell(k, it):
        rows = slice(256 * it, 256 * it + 256)
        product = lax.dot_general(share_ref[...], kcell_ref[k, rows, :], NT, preferred_element_type=F32)
        cells[it].append(load_sum(product * fpack_ref[:, rows].astype(F32), 256))

    def row_node(k, it):
        rows = slice(256 * it, 256 * it + 256)
        product = lax.dot_general(nhalf_ref[it], knode_ref[k, rows, :], NT, preferred_element_type=F32)
        value = load_sum(product * fpack_ref[:, rows].astype(F32), 256)
        pieces[it].append(-(value + 3.0 * cells[it][k]))

    for it in range(4):
        few = [lambda k=k, it=it: row_cell(k, it - 1) for k in range(3)] if it else []
        weave([lambda s=s, jt=jt, it=it: cell_fill(16 * it + s, jt) for s in range(16) for jt in range(4)], few)
    many = [lambda s=s: mark(s) for s in range(32)] + [lambda jt=jt: part(jt) for jt in range(4)]
    for s in range(64):
        many += [lambda s=s, h=h: node_fill(s, h) for h in range(2)]
        if s % 3 == 0 and s // 3 < 18:
            many.append(lambda s=s: blend(s // 3))
    weave(
        many,
        [lambda k=k: row_cell(k, 3) for k in range(3)]
        + [lambda k=k, jt=jt: cell_dot(k, jt) for jt in range(4) for k in range(3)],
    )
    for it in range(4):
        for k in range(3):
            node_dot(k, it)
            row_node(k, it)
    nodes = jnp.concatenate([part[0] + part[1] + part[2] + part[3] for part in nodes], 0)
    value = elem_ref[...]
    high = value.astype(BF)
    low = (value - high.astype(F32)).astype(BF)
    spread = lax.dot_general(
        jnp.concatenate([high, low], 0), touch_ref[...], NT, preferred_element_type=F32
    )
    node_ref[...] = (nodes + (spread[:48] + spread[48:])).astype(BF)

    columns = []
    for it in range(4):
        filled = jnp.concatenate(pieces[it] + [jnp.zeros((80, 256), F32)], 0)
        columns.append(jnp.transpose(filled))
    turned = jnp.concatenate(columns, 0).reshape(64, 16, 128)
    packed = turned[:, :8] + pltpu.roll(turned[:, 8:].reshape(512, 128), 64, 1).reshape(64, 8, 128)
    front_ref[...] = packed.astype(BF)


def last_kernel(front_ref, own_ref, core_ref, side_ref, cross_ref, out_front_ref, out_node_ref):
    total = jnp.sum(front_ref[...].astype(F32), axis=0)
    out_front_ref[0:8, :] = total[:, 0:48]
    out_front_ref[8:16, :] = pltpu.roll(total, 64, 1)[:, 0:48]
    near = own_ref[...].astype(F32) + core_ref[...].astype(F32)
    far = side_ref[...].astype(F32) + cross_ref[...].astype(F32)
    out_node_ref[...] = near + far


def shape(dims, dtype):
    return jax.ShapeDtypeStruct(dims, dtype)


VMEM = pl.BlockSpec(memory_space=pltpu.VMEM)
SMEM = pl.BlockSpec(memory_space=pltpu.SMEM)


def body(state, adjoint, area, node_coords, connect, front_list, tile_class):
    col = lax.axis_index(COL).astype(jnp.int32).reshape(1)
    front_list = front_list.reshape(1, 1024)
    owners = (front_list >> 8).astype(BF)
    mine = jnp.concatenate([state.T, adjoint.T, owners, jnp.zeros((7, 1024), BF)], 0)
    gathered = lax.all_gather(mine, ROW)
    pack, points, table, pool, place, fits = pl.pallas_call(
        prep_kernel,
        out_shape=(
            shape((288, 1024), BF),
            shape((16, 1024), F32),
            shape((304, 1024), BF),
            shape((8, 2 * CAP + CAP_PART, 128), BF),
            shape((2, 1024), jnp.int32),
            shape((1, 1), jnp.int32),
        ),
        in_specs=[SMEM] + [VMEM] * 4,
        out_specs=(VMEM, VMEM, VMEM, VMEM, VMEM, SMEM),
        compiler_params=pltpu.CompilerParams(vmem_limit_bytes=24 << 20),
        name="prep",
    )(col, gathered, connect, node_coords, front_list)

    def compact(pool, place, table):
        part = lax.all_to_all(pool, "z", 0, 0)
        merged = pl.pallas_call(
            merge_kernel,
            out_shape=shape((8, 2 * SLOTS + SLOT_PART, 128), BF),
            in_specs=[SMEM] + [VMEM] * 2,
            out_specs=VMEM,
            compiler_params=pltpu.CompilerParams(vmem_limit_bytes=24 << 20),
            name="merge",
        )(col, part, place)
        return lax.all_to_all(merged, ("yh", "x"), 0, 0), place

    def whole(pool, place, table):
        rows = pl.pallas_call(
            whole_kernel,
            out_shape=shape((1024, 384), BF),
            in_specs=[SMEM] + [VMEM] * 2,
            out_specs=VMEM,
            name="whole",
        )(col, table, front_list)
        part = lax.all_to_all(rows.reshape(64, 16, 384), COL, 0, 0)
        share = jnp.sum(part, axis=0, dtype=BF)
        spread = jnp.broadcast_to(share[None], (64, 16, 384))
        rows = lax.all_to_all(spread, COL, 0, 0).reshape(1024, 384)
        rows = jnp.pad(rows, ((0, 8 * SLOTS - 1024), (0, 0))).reshape(8, SLOTS, 384)
        third = jnp.pad(rows[:, :, 256:298], ((0, 0), (0, 3 * SLOT_PART - SLOTS), (0, 0)))
        third = third.reshape(8, 3, SLOT_PART, 42)
        third = jnp.concatenate([third[:, 0], third[:, 1], third[:, 2]], 2)
        third = jnp.pad(third, ((0, 0), (0, 0), (0, 2)))
        pool = jnp.concatenate([rows[:, :, 0:128], rows[:, :, 128:256], third], 1)
        return pool, jnp.broadcast_to(jnp.arange(1024, dtype=jnp.int32), (2, 1024))

    fronts, slots = lax.cond(fits[0, 0] == FAST, compact, whole, pool, place, table)
    front_part, node_part = pl.pallas_call(
        main_kernel,
        out_shape=(shape((64, 8, 128), BF), shape((48, 512), BF)),
        in_specs=[SMEM] * 2 + [VMEM] * 7,
        out_specs=(VMEM, VMEM),
        scratch_shapes=[
            pltpu.VMEM((3, 1024, 512), BF),
            pltpu.VMEM((3, 1024, 1024), BF),
            pltpu.VMEM((3, 1024, 128), F32),
            pltpu.VMEM((288, 1024), BF),
            pltpu.VMEM((288, 1024), BF),
            pltpu.VMEM((512, 1024), BF),
            pltpu.VMEM((4, 288, 512), F32),
            pltpu.VMEM((4, 288, 512), F32),
            pltpu.VMEM((4, 288, 512), BF),
            pltpu.VMEM((48, 1024), F32),
            pltpu.VMEM((3, 8, 1536), F32),
        ],
        compiler_params=pltpu.CompilerParams(vmem_limit_bytes=44 << 20),
        name="sweep",
    )(
        col,
        tile_class,
        pack,
        points,
        area.reshape(1, 1024),
        connect,
        node_coords,
        fronts,
        slots,
    )
    core = lax.ppermute(node_part, ROW, [(i, i ^ 1) for i in range(4)])
    side = lax.ppermute(node_part, ROW, [(i, i ^ 2) for i in range(4)])
    cross = lax.ppermute(node_part, ROW, [(i, i ^ 3) for i in range(4)])
    front_sum = lax.all_to_all(front_part, COL, 0, 0)
    front_grad, node_grad = pl.pallas_call(
        last_kernel,
        out_shape=(shape((16, 48), F32), shape((48, 512), F32)),
        in_specs=[VMEM] * 5,
        out_specs=(VMEM, VMEM),
        compiler_params=pltpu.CompilerParams(vmem_limit_bytes=16 << 20),
        name="last",
    )(front_sum, node_part, core, side, cross)
    return (front_grad, node_grad.T)


def solution(mesh):
    fine = Mesh(mesh.devices.reshape(2, 2, 8, 2, 4), ROW + COL)
    in_specs = (
        P(COL, ROW),
        P(COL, ROW),
        P(COL),
        P(None, COL),
        P(None, COL),
        P(ROW),
        P(ROW, COL),
    )
    out_specs = (P(ROW + COL, None), P(COL, None))
    return jax.shard_map(body, mesh=fine, in_specs=in_specs, out_specs=out_specs, check_vma=False)
```
